256 devices in a mesh: prog: 32 (over z, x), clus: 8 (over y, core).
Axes of the slice: x: 4, y: 4, z: 8, core: 2. Of those that a mesh axis runs over, the one named last changes fastest.
Arguments:
- embeddings: bfloat16 [32768, 2048], P('prog', 'clus'), may hold values from -64 to 64, as said below
- centroids: bfloat16 [4096, 2048], P('clus'), may hold values from -6 to 6, as said below
- plan_grad: bfloat16 [32768, 4096], P('prog', 'clus'), may hold values from -24 to 24
Outputs:
- embed_grad: bfloat16 [32768, 2048], P('prog', 'clus')
- centroid_grad: bfloat16 [4096, 2048], P(('clus', 'prog'))
The draws below stay inside these ranges and needn't reach their ends.
Inputs may be any that keep to these rules, and one draw needn't show every extreme that they name: embeddings are real-valued with full-rank spread. centroids are real-valued with full-rank spread.
All inputs are finite; a program needn't handle non-finite values.
Results may differ from the reference program's by a relative error of at most 0.006.
Values may be sent and summed in bfloat16 or wider, within the bound.
No kernel may reach another device: no remote copies, remote signals or barrier semaphores. Data moves between devices by JAX's collectives and lax.ppermute only.
A program may use at most 64 MiB of HBM per device.

```python
import jax
import jax.numpy as jnp
from jax import lax

D = 2048
CENTROIDS = 4096
ITERS = 4
TOTAL = 32768


def draw_common(key):
    cent = jnp.clip(jax.random.normal(jax.random.fold_in(key, 7), (CENTROIDS, D), jnp.float32), -6.0, 6.0)
    embed = 2.0 * jnp.clip(jax.random.normal(jax.random.fold_in(key, 11), (TOTAL, D), jnp.float32), -6.0, 6.0)
    dead = jax.random.randint(jax.random.fold_in(key, 29), (), 0, CENTROIDS)
    cent = cent.at[dead].set(-6.0)
    aligned = min(64, TOTAL // 2)
    pick_one = jax.random.randint(jax.random.fold_in(key, 19), (aligned,), 1, CENTROIDS)
    offset = jax.random.randint(jax.random.fold_in(key, 23), (aligned,), 1, CENTROIDS - 1)
    pick_two = 1 + (pick_one - 1 + offset) % (CENTROIDS - 1)
    first = (dead + pick_one) % CENTROIDS
    second = (dead + pick_two) % CENTROIDS
    strength = jnp.array([0.6, 0.9, 1.2], jnp.float32)[jnp.arange(aligned) % 3][:, None]
    lift = 50.0 / jnp.sqrt(jnp.float32(D))
    mixed = strength * (cent[first] + 0.99 * cent[second]) * lift
    embed = embed.at[:aligned].set(mixed)
    embed = jnp.clip(embed + 2.0, -64.0, 64.0)
    return (embed, cent)


def draw_embeddings(key, part):
    return draw_common(key)[0].astype(jnp.bfloat16)


def draw_centroids(key, part):
    return draw_common(key)[1].astype(jnp.bfloat16)


def strengthened(result, stream_key, source, target, parts, factor):
    def block_of(position):
        return (jnp.arange(result.shape[position]) // (result.shape[position] // parts)).reshape((-1,) + (1,) * (result.ndim - 1 - position))

    one_side = jax.random.permutation(stream_key, parts)[block_of(target)]
    far = (block_of(target) + parts // 2) % parts
    return jnp.where((block_of(source) == one_side) | (block_of(source) == far), factor * result, result)


def block_levels(stream_key, extent, split, low, top_value):
    def one(dim, blocks):
        steps = jax.random.uniform(jax.random.fold_in(jax.random.fold_in(stream_key, 6), dim), (blocks,), jnp.float32, low / len(split), top_value / len(split))
        return jnp.repeat(jnp.exp(steps), extent[dim] // blocks).reshape((-1,) + (1,) * (len(extent) - dim - 1))

    factor_of = one(*split[0])
    for cut in split[1:]:
        factor_of = factor_of * one(*cut)
    return factor_of


def noise_with(rng, dims, width, most, cuts, heavy, kind=jnp.bfloat16):
    entries = width * jax.random.normal(rng, dims, jnp.float32)
    if cuts:
        entries = entries * block_levels(rng, dims, cuts, -0.22, 0.18)
    return jnp.clip(strengthened(entries, jax.random.fold_in(rng, 3), *heavy), -most, most).astype(kind)


def setup_inputs(seed: int = 0) -> dict:
    splits = jax.random.split(jax.random.key(seed), 4)
    return {
        "embeddings": draw_embeddings(jax.random.fold_in(splits[3], 71), 0),
        "centroids": draw_centroids(jax.random.fold_in(splits[3], 71), 0),
        "plan_grad": noise_with(splits[2], (TOTAL, CENTROIDS), 4.0, 24.0, ((0, 32), (1, 8)), (0, 1, 32, 2.75)),
    }


def lse_along(values, axis):
    top = lax.optimization_barrier(jnp.max(values, axis=axis, keepdims=True))
    total = lax.optimization_barrier(jnp.sum(jnp.exp(values - top), axis=axis, keepdims=True))
    return jnp.squeeze(top + jnp.log(total), axis)

def reference(embeddings, centroids, plan_grad):
    scale = 1.0 / (0.25 * jnp.sqrt(jnp.float32(D)))
    logits = scale * lax.dot_general(embeddings, centroids, (((1,), (1,)), ((), ())), preferred_element_type=jnp.float32)
    log_b = jnp.log(jnp.float32(TOTAL) / jnp.float32(CENTROIDS))
    col_pot = jnp.zeros((CENTROIDS,), jnp.float32)
    row_list = []
    col_list = []
    for step in range(ITERS):
        row_pot = -lse_along(logits + col_pot[None, :], 1)
        col_pot = log_b - lse_along(logits + row_pot[:, None], 0)
        row_list.append(row_pot)
        col_list.append(col_pot)
    plan = jnp.exp(logits + row_list[-1][:, None] + col_list[-1][None, :])
    pbar = plan_grad.astype(jnp.float32) * plan
    adjoint = pbar
    col_adj = lax.optimization_barrier(jnp.sum(pbar, axis=0))
    direct = lax.optimization_barrier(jnp.sum(pbar, axis=1))
    for step in range(ITERS - 1, -1, -1):
        weights_a = jnp.exp(logits + row_list[step][:, None] + col_list[step][None, :] - log_b)
        term_a = weights_a * col_adj[None, :]
        adjoint = adjoint - term_a
        row_adj = direct - lax.optimization_barrier(jnp.sum(term_a, axis=1))
        direct = jnp.zeros_like(direct)
        if step > 0:
            prev_col = col_list[step - 1]
        else:
            prev_col = jnp.zeros((CENTROIDS,), jnp.float32)
        term_b = jnp.exp(logits + prev_col[None, :] + row_list[step][:, None]) * row_adj[:, None]
        adjoint = adjoint - term_b
        if step > 0:
            col_adj = -lax.optimization_barrier(jnp.sum(term_b, axis=0))
    adjoint_b = adjoint.astype(jnp.bfloat16)
    embed_grad = (scale * jnp.dot(adjoint_b, centroids, preferred_element_type=jnp.float32)).astype(jnp.bfloat16)
    centroid_grad = (scale * lax.dot_general(adjoint_b, embeddings, (((0,), (0,)), ((), ())), preferred_element_type=jnp.float32)).astype(jnp.bfloat16)
    return (embed_grad, centroid_grad)
```

```python
import functools
import math

import jax
import jax.numpy as jnp
from jax import lax
from jax.experimental import pallas as pl
from jax.experimental.pallas import tpu as pltpu
from jax.sharding import Mesh
from jax.sharding import PartitionSpec as P

ITERS = 4
L = 128
F32 = jnp.float32
BF16 = jnp.bfloat16
NT = (((1,), (1,)), ((), ()))
NN = (((1,), (0,)), ((), ()))
TN = (((0,), (0,)), ((), ()))
SMALL = 12 << 20
LARGE = 40 << 20


def spread(vec):
    parts = [jnp.broadcast_to(vec[q : q + 1, :], (L, L)).T for q in range(vec.shape[0])]
    return jnp.concatenate(parts, axis=0)


def put_rows(out, parts):
    whole = jnp.concatenate(parts, axis=0)
    out[...] = jnp.broadcast_to(whole[None], out.shape)


def row_sums(values):
    return [jnp.sum(v, axis=0, keepdims=True) for v in values]


def gather_cols(part):
    return jnp.concatenate(
        [
            jnp.sum(part[q * L : (q + 1) * L, :].T, axis=0, keepdims=True)
            for q in range(part.shape[0] // L)
        ],
        axis=0,
    )


def first_lane(part):
    return jnp.concatenate(
        [part[q * L : (q + 1) * L, :].T[0:1, :] for q in range(part.shape[0] // L)], axis=0
    )


def lanes(ref, r):
    return ref[:, r * L : (r + 1) * L]


def total(recv):
    return jnp.sum(recv[...], axis=0)


def merge(recv):
    tops = recv[:, 0]
    top = jnp.max(tops, axis=0)
    return top + jnp.log(jnp.sum(recv[:, 1] * jnp.exp(tops - top[None]), axis=0))


def k_logits(scale, where, cent, *refs):
    n = len(refs) - 3
    pieces, (whole, logits, send) = refs[:n], refs[n:]
    width = pieces[0].shape[1]
    for k in range(n):
        whole[:, pl.ds(pl.multiple_of(where[k] * width, L), width)] = pieces[k][...]
    logits[...] = scale * lax.dot_general(cent[...], whole[...], NT, preferred_element_type=F32)
    count = logits.shape[1] // L
    tops, sums = [], []
    for r in range(count):
        tile = lanes(logits, r)
        top = jnp.max(tile, axis=0, keepdims=True)
        tops.append(top)
        sums.append(jnp.sum(jnp.exp(tile - top), axis=0, keepdims=True))
    send[:, 0] = jnp.broadcast_to(jnp.concatenate(tops, axis=0)[None], send[:, 0].shape)
    send[:, 1] = jnp.broadcast_to(jnp.concatenate(sums, axis=0)[None], send[:, 1].shape)


def k_first_col(logits, recv, row_pot, send):
    u = -merge(recv)
    row_pot[...] = u
    count = u.shape[0]
    top = lanes(logits, 0) + u[0:1, :]
    for r in range(1, count):
        top = jnp.maximum(top, lanes(logits, r) + u[r : r + 1, :])
    top = jnp.broadcast_to(jnp.max(top, axis=1, keepdims=True), top.shape)
    part = jnp.exp(lanes(logits, 0) + u[0:1, :] - top)
    for r in range(1, count):
        part = part + jnp.exp(lanes(logits, r) + u[r : r + 1, :] - top)
    send[:, 0] = jnp.broadcast_to(first_lane(top)[None], send[:, 0].shape)
    send[:, 1] = jnp.broadcast_to(gather_cols(part)[None], send[:, 1].shape)


def k_weights(log_b, logits, row_pot, recv, col_pot, weights, send):
    v = log_b - merge(recv)
    col_pot[...] = v
    vv = spread(v)
    u = row_pot[...]
    out = []
    for r in range(u.shape[0]):
        tile = jnp.exp(lanes(logits, r) + u[r : r + 1, :] + vv)
        weights[:, r * L : (r + 1) * L] = tile
        out.append(jnp.sum(tile, axis=0, keepdims=True))
    put_rows(send, out)


def weighted(weights, vec):
    part = lanes(weights, 0) * vec[0:1, :]
    for r in range(1, vec.shape[0]):
        part = part + lanes(weights, r) * vec[r : r + 1, :]
    return part


def k_col(weights, recv, row_mul, send):
    a = 1.0 / total(recv)
    row_mul[...] = a
    send[...] = jnp.broadcast_to(gather_cols(weighted(weights, a))[None], send.shape)


def k_row(ratio, weights, recv, col_mul, send):
    b = ratio / total(recv)
    col_mul[...] = b
    bb = spread(b)
    count = weights.shape[1] // L
    put_rows(send, row_sums([lanes(weights, r) * bb for r in range(count)]))


def k_last_col(weights, grad, recv, row_mul, send):
    a = 1.0 / total(recv)
    row_mul[...] = a
    part = lanes(weights, 0) * a[0:1, :]
    bar = part * lanes(grad, 0).astype(F32)
    for r in range(1, a.shape[0]):
        step = lanes(weights, r) * a[r : r + 1, :]
        part = part + step
        bar = bar + step * lanes(grad, r).astype(F32)
    send[:, 0] = jnp.broadcast_to(gather_cols(part)[None], send[:, 0].shape)
    send[:, 1] = jnp.broadcast_to(gather_cols(bar)[None], send[:, 1].shape)


def k_adj_row(ratio, weights, grad, recv, col_mul, col_adj, send):
    sums = total(recv)
    b = ratio / sums[0]
    x = b * (b * sums[1]) / ratio
    col_mul[...] = b
    col_adj[...] = x
    bb, xx = spread(b), spread(x)
    count = weights.shape[1] // L
    put_rows(
        send,
        row_sums(
            [lanes(weights, r) * (bb * lanes(grad, r).astype(F32) - xx) for r in range(count)]
        ),
    )


def k_back_col(sign, weights, row_mul, recv, row_adj, send):
    a = row_mul[...]
    y = sign * a * a * total(recv)
    row_adj[...] = y
    send[...] = jnp.broadcast_to(gather_cols(weighted(weights, y))[None], send.shape)


def k_back_row(ratio, weights, col_mul, recv, col_adj, send):
    b = col_mul[...]
    x = -b * b * total(recv) / ratio
    col_adj[...] = x
    xx = spread(x)
    count = weights.shape[1] // L
    put_rows(send, row_sums([lanes(weights, r) * xx for r in range(count)]))


def k_adjoint(scale, where, weights, grad, cent, col_pot, *refs):
    n = ITERS - 1
    row_mul = [None] + [r[...] for r in refs[:n]]
    col_mul = [jnp.exp(-col_pot[...]), None] + [r[...] for r in refs[n : 2 * n]]
    x = [r[...] for r in refs[2 * n : 3 * n + 1]]
    y = [None] + [r[...] for r in refs[3 * n + 1 : 4 * n + 1]]
    recv, adjoint, keep, cross = refs[4 * n + 1 :]
    y[0] = -total(recv)
    b4 = spread(col_mul[ITERS])
    xs = [spread(v) for v in x]
    bs = [spread(col_mul[0]), None] + [spread(v) for v in col_mul[2:ITERS]]
    count = y[0].shape[0]
    for r in range(count):
        row = slice(r, r + 1)
        inner = (b4 * row_mul[n][row, :]) * lanes(grad, r).astype(F32) - xs[0] - y[1][row, :]
        inner = inner - bs[0] * y[0][row, :]
        for t in range(1, ITERS):
            inner = inner - xs[t] * row_mul[t][row, :]
        for t in range(2, ITERS):
            inner = inner - bs[t] * y[t][row, :]
        adjoint[:, r * L : (r + 1) * L] = (lanes(weights, r) * inner).astype(BF16)
    width = keep.shape[2]
    for k in range(keep.shape[0]):
        for out, at in ((cross, where[1, k]), (keep, where[0, k])):
            block = cent[:, pl.ds(pl.multiple_of(at * width, L), width)]
            out[k] = (
                scale * lax.dot_general(adjoint[...], block, TN, preferred_element_type=F32)
            ).astype(out.dtype)


def k_cent(scale, groups, adjoint, whole, out):
    xs, zs, rows, _ = out.shape
    half = whole.shape[1] // 2
    for h in range(2):
        cols = slice(h * half, (h + 1) * half)
        part = scale * lax.dot_general(
            adjoint[...], whole[:, cols], NN, preferred_element_type=F32
        )
        part = part.astype(BF16)
        for iz in range(zs):
            for ix in range(xs):
                at = (iz * xs + ix) * rows
                out[ix, iz, :, cols] = part[at : at + rows, :]


def call(body, outs, *args, limit=SMALL, scalars=0, flops=0):
    spec = pl.BlockSpec(memory_space=pltpu.VMEM)
    ins = [pl.BlockSpec(memory_space=pltpu.SMEM)] * scalars + [spec] * (len(args) - scalars)
    size = sum(a.size * a.dtype.itemsize for a in args)
    return pl.pallas_call(
        body,
        out_shape=[jax.ShapeDtypeStruct(s, d) for s, d in outs],
        in_specs=ins,
        out_specs=[spec] * len(outs),
        compiler_params=pltpu.CompilerParams(vmem_limit_bytes=limit),
        cost_estimate=pl.CostEstimate(flops=flops, bytes_accessed=size, transcendentals=0),
        name=getattr(body, "func", body).__name__,
    )(*args)


def shift(value, axis, step):
    n = lax.axis_size(axis)
    return lax.ppermute(value, axis, [(i, (i + step) % n) for i in range(n)])


def shards(embeddings, centroids, plan_grad):
    rows, width = embeddings.shape
    cols, depth = centroids.shape
    ny, nx, nz = lax.axis_size("y"), lax.axis_size("x"), lax.axis_size("z")
    nclus, nprog = ny * 2, nz * nx
    scale = 1.0 / (0.25 * float(depth) ** 0.5)
    ratio = (rows * nprog) / (cols * nclus)
    log_b = math.log(ratio)
    rv, cv = (rows // L, L), (cols // L, L)
    iy, ic = lax.axis_index("y"), lax.axis_index("core")

    mine = [embeddings] + [shift(embeddings, "y", k) for k in range(1, ny)]
    theirs = [shift(m, "core", 1) for m in mine]
    source = [lax.rem(iy - k + ny, ny) * 2 for k in range(ny)]
    where = jnp.stack([s + ic for s in source] + [s + 1 - ic for s in source]).astype(jnp.int32)
    grad = plan_grad.T

    def over_clus(send):
        return lax.all_to_all(send, ("y", "core"), 0, 0, tiled=True)

    def over_prog(send):
        return lax.all_to_all(send, ("z", "x"), 0, 0, tiled=True)

    block = ((cols, rows), F32)
    row_send, col_send = ((nclus, *rv), F32), ((nprog, *cv), F32)
    row_pair, col_pair = ((nclus, 2, *rv), F32), ((nprog, 2, *cv), F32)
    a_row, a_col = (rv, F32), (cv, F32)

    whole, logits, send = call(
        functools.partial(k_logits, scale),
        [((rows, depth), BF16), block, row_pair],
        where, centroids, *mine, *theirs,
        limit=LARGE, scalars=1, flops=2 * rows * cols * depth,
    )
    row_pot, send = call(k_first_col, [a_row, col_pair], logits, over_clus(send))
    col_pot, weights, send = call(
        functools.partial(k_weights, log_b), [a_col, block, row_send], logits, row_pot, over_prog(send)
    )
    row_mul, col_mul = [], []
    for step in range(1, ITERS):
        recv = over_clus(send)
        if step < ITERS - 1:
            a, send = call(k_col, [a_row, col_send], weights, recv)
            b, send = call(
                functools.partial(k_row, ratio), [a_col, row_send], weights, over_prog(send)
            )
            col_mul.append(b)
        else:
            a, send = call(k_last_col, [a_row, col_pair], weights, grad, recv)
        row_mul.append(a)
    b, x, send = call(
        functools.partial(k_adj_row, ratio),
        [a_col, a_col, row_send],
        weights, grad, over_prog(send),
    )
    col_mul.append(b)
    col_adj, row_adj = [x], []
    for step in range(ITERS - 1, 0, -1):
        y, send = call(
            functools.partial(k_back_col, 1.0 if step == ITERS - 1 else -1.0),
            [a_row, col_send],
            weights, row_mul[step - 1], over_clus(send),
        )
        row_adj.insert(0, y)
        b = col_mul[step - 2] if step > 1 else jnp.ones(cv, F32)
        x, send = call(
            functools.partial(k_back_row, ratio), [a_col, row_send], weights, b, over_prog(send)
        )
        col_adj.insert(0, x)

    target = [lax.rem(iy + k, ny) * 2 for k in range(ny)]
    slots = jnp.stack(
        [jnp.stack([s + ic for s in target]), jnp.stack([s + 1 - ic for s in target])]
    ).astype(jnp.int32)
    adjoint, keep, cross = call(
        functools.partial(k_adjoint, scale),
        [((cols, rows), BF16), ((ny, rows, width), F32), ((ny, rows, width), BF16)],
        slots, weights, grad, centroids, col_pot, *row_mul, *col_mul, *col_adj, *row_adj, over_clus(send),
        limit=LARGE, scalars=1, flops=2 * rows * cols * depth,
    )
    cross = shift(cross, "core", 1)
    (parts,) = call(
        functools.partial(k_cent, scale, nx),
        [((nx, nz, cols // nprog, depth), BF16)],
        adjoint, whole,
        limit=LARGE, flops=2 * rows * cols * depth,
    )
    both = [keep[k] + cross[k].astype(F32) for k in range(ny)]
    moved = [shift(both[k].astype(BF16), "y", k) for k in range(1, ny)]
    parts = lax.all_to_all(parts, "x", 0, 0, tiled=True)
    parts = jnp.sum(parts.astype(F32), axis=0).astype(BF16)
    parts = lax.all_to_all(parts, "z", 0, 0, tiled=True)
    centroid_grad = jnp.sum(parts.astype(F32), axis=0).astype(BF16)
    embed_grad = both[0]
    for m in moved:
        embed_grad = embed_grad + m.astype(F32)
    return embed_grad.astype(BF16), centroid_grad


def solution(mesh):
    shape = dict(mesh.shape)
    nx = 4 if shape["prog"] % 4 == 0 and shape["prog"] > 4 else 2
    grid = (shape["prog"] // nx, nx, shape["clus"] // 2, 2)
    fine = Mesh(mesh.devices.reshape(grid), ("z", "x", "y", "core"))
    prog, clus = ("z", "x"), ("y", "core")
    return jax.shard_map(
        shards,
        mesh=fine,
        in_specs=(P(prog, clus), P(clus, None), P(prog, clus)),
        out_specs=(P(prog, clus), P(clus + prog, None)),
        check_vma=False,
    )
```

```python
import functools
import math

import jax
import jax.numpy as jnp
from jax import lax
from jax.experimental import pallas as pl
from jax.experimental.pallas import tpu as pltpu
from jax.sharding import Mesh
from jax.sharding import PartitionSpec as P


ITERS = 4
L = 128
F32 = jnp.float32
BF16 = jnp.bfloat16
NT = (((1,), (1,)), ((), ()))
NN = (((1,), (0,)), ((), ()))
SMALL = 12 << 20
LARGE = 40 << 20


def spread(vec):
    parts = [jnp.broadcast_to(vec[q : q + 1, :], (L, L)).T for q in range(vec.shape[0])]
    return jnp.concatenate(parts, axis=0)


def put_rows(out, parts):
    whole = jnp.concatenate(parts, axis=0)
    out[...] = jnp.broadcast_to(whole[None], out.shape)


def row_sums(values):
    return [jnp.sum(v, axis=0, keepdims=True) for v in values]


def gather_cols(part):
    return jnp.concatenate(
        [
            jnp.sum(part[q * L : (q + 1) * L, :].T, axis=0, keepdims=True)
            for q in range(part.shape[0] // L)
        ],
        axis=0,
    )


def first_lane(part):
    return jnp.concatenate(
        [part[q * L : (q + 1) * L, :].T[0:1, :] for q in range(part.shape[0] // L)], axis=0
    )


def lanes(ref, r):
    return ref[:, r * L : (r + 1) * L]


def total(recv):
    return jnp.sum(recv[...], axis=0)


def merge(recv):
    tops = recv[:, 0]
    top = jnp.max(tops, axis=0)
    return top + jnp.log(jnp.sum(recv[:, 1] * jnp.exp(tops - top[None]), axis=0))


def k_prepare(plan_grad, grad):
    grad[...] = plan_grad[...].T


def k_logits(scale, where, cent, *refs):
    n = len(refs) - 4
    pieces, (logits, send, held, sems) = refs[:n], refs[n:]
    width = pieces[0].shape[1]
    copies = [
        pltpu.make_async_copy(
            piece, held.at[:, pl.ds(pl.multiple_of(where[k] * width, L), width)], sems.at[k]
        )
        for k, piece in enumerate(pieces)
    ]
    for c in copies:
        c.start()
    for c in copies:
        c.wait()
    logits[...] = scale * lax.dot_general(cent[...], held[...], NT, preferred_element_type=F32)
    count = logits.shape[1] // L
    tops, sums = [], []
    for r in range(count):
        tile = lanes(logits, r)
        top = jnp.max(tile, axis=0, keepdims=True)
        tops.append(top)
        sums.append(jnp.sum(jnp.exp(tile - top), axis=0, keepdims=True))
    send[:, 0] = jnp.broadcast_to(jnp.concatenate(tops, axis=0)[None], send[:, 0].shape)
    send[:, 1] = jnp.broadcast_to(jnp.concatenate(sums, axis=0)[None], send[:, 1].shape)


def k_first_col(logits, recv, row_pot, send):
    u = -merge(recv)
    row_pot[...] = u
    count = u.shape[0]
    top = lanes(logits, 0) + u[0:1, :]
    for r in range(1, count):
        top = jnp.maximum(top, lanes(logits, r) + u[r : r + 1, :])
    top = jnp.broadcast_to(jnp.max(top, axis=1, keepdims=True), top.shape)
    part = jnp.exp(lanes(logits, 0) + u[0:1, :] - top)
    for r in range(1, count):
        part = part + jnp.exp(lanes(logits, r) + u[r : r + 1, :] - top)
    send[:, 0] = jnp.broadcast_to(first_lane(top)[None], send[:, 0].shape)
    send[:, 1] = jnp.broadcast_to(gather_cols(part)[None], send[:, 1].shape)


def k_weights(log_b, logits, row_pot, recv, col_pot, weights, send):
    v = log_b - merge(recv)
    col_pot[...] = v
    vv = spread(v)
    u = row_pot[...]
    out = []
    for r in range(u.shape[0]):
        tile = jnp.exp(lanes(logits, r) + u[r : r + 1, :] + vv)
        weights[:, r * L : (r + 1) * L] = tile
        out.append(jnp.sum(tile, axis=0, keepdims=True))
    put_rows(send, out)


def weighted(weights, vec):
    part = lanes(weights, 0) * vec[0:1, :]
    for r in range(1, vec.shape[0]):
        part = part + lanes(weights, r) * vec[r : r + 1, :]
    return part


def k_col(weights, recv, row_mul, send):
    a = 1.0 / total(recv)
    row_mul[...] = a
    send[...] = jnp.broadcast_to(gather_cols(weighted(weights, a))[None], send.shape)


def k_row(ratio, weights, recv, col_mul, send):
    b = ratio / total(recv)
    col_mul[...] = b
    bb = spread(b)
    count = weights.shape[1] // L
    put_rows(send, row_sums([lanes(weights, r) * bb for r in range(count)]))


def k_last_col(weights, grad, recv, row_mul, send):
    a = 1.0 / total(recv)
    row_mul[...] = a
    part = lanes(weights, 0) * a[0:1, :]
    bar = part * lanes(grad, 0).astype(F32)
    for r in range(1, a.shape[0]):
        step = lanes(weights, r) * a[r : r + 1, :]
        part = part + step
        bar = bar + step * lanes(grad, r).astype(F32)
    send[:, 0] = jnp.broadcast_to(gather_cols(part)[None], send[:, 0].shape)
    send[:, 1] = jnp.broadcast_to(gather_cols(bar)[None], send[:, 1].shape)


def k_adj_row(ratio, weights, grad, recv, col_mul, col_adj, send):
    sums = total(recv)
    b = ratio / sums[0]
    x = b * (b * sums[1]) / ratio
    col_mul[...] = b
    col_adj[...] = x
    bb, xx = spread(b), spread(x)
    count = weights.shape[1] // L
    put_rows(
        send,
        row_sums(
            [lanes(weights, r) * (bb * lanes(grad, r).astype(F32) - xx) for r in range(count)]
        ),
    )


def k_back_col(sign, weights, row_mul, recv, row_adj, send):
    a = row_mul[...]
    y = sign * a * a * total(recv)
    row_adj[...] = y
    send[...] = jnp.broadcast_to(gather_cols(weighted(weights, y))[None], send.shape)


def k_back_row(ratio, weights, col_mul, recv, col_adj, send):
    b = col_mul[...]
    x = -b * b * total(recv) / ratio
    col_adj[...] = x
    xx = spread(x)
    count = weights.shape[1] // L
    put_rows(send, row_sums([lanes(weights, r) * xx for r in range(count)]))


def k_known(weights, grad, col_pot, *refs):
    n = ITERS - 1
    base, first = refs[4 * n + 1 :]
    row_mul = [None] + [r[...] for r in refs[:n]]
    col_mul = [None, None] + [r[...] for r in refs[n : 2 * n]]
    x = [r[...] for r in refs[2 * n : 3 * n + 1]]
    y = [None] + [r[...] for r in refs[3 * n + 1 : 4 * n + 1]]
    b0 = spread(jnp.exp(-col_pot[...]))
    b4 = spread(col_mul[ITERS])
    xs = [spread(v) for v in x]
    bs = [None, None] + [spread(v) for v in col_mul[2:ITERS]]
    for r in range(base.shape[1] // L):
        row = slice(r, r + 1)
        tile = lanes(weights, r)
        inner = (b4 * row_mul[n][row, :]) * lanes(grad, r).astype(F32) - xs[0] - y[1][row, :]
        for t in range(1, ITERS):
            inner = inner - xs[t] * row_mul[t][row, :]
        for t in range(2, ITERS):
            inner = inner - bs[t] * y[t][row, :]
        first[:, r * L : (r + 1) * L] = (tile * b0).astype(BF16)
        base[:, r * L : (r + 1) * L] = tile * inner


def k_adjoint(scale, where, order, base, first, recv, *refs):
    n = where.shape[0]
    nx = order.shape[0]
    pieces, adjoint, keep = refs[:n], refs[n], refs[n + 1]
    sends, (held, turned, sems) = refs[n + 2 : n + 1 + nx], refs[n + 1 + nx :]
    copies = [
        pltpu.make_async_copy(piece, held.at[k], sems.at[k]) for k, piece in enumerate(pieces)
    ]
    for c in copies:
        c.start()
    y = -total(recv)
    for r in range(y.shape[0]):
        adjoint[:, r * L : (r + 1) * L] = (
            lanes(base, r) - lanes(first, r).astype(F32) * y[r : r + 1, :]
        ).astype(BF16)
    per = keep.shape[0]
    group = 16
    for k in range(nx):
        for iz in range(per // group):
            at = pl.multiple_of((iz * nx + order[k]) * group, group)
            turned[k * per + iz * group : k * per + (iz + 1) * group, :] = adjoint[pl.ds(at, group), :]
    width = held.shape[2]
    for p in range(n):
        copies[p].wait()
        part = scale * lax.dot_general(turned[...], held[p], NN, preferred_element_type=F32)
        cols = pl.ds(pl.multiple_of(where[p] * width, L), width)
        keep[:, cols] = part[:per, :]
        for k in range(1, nx):
            sends[k - 1][:, cols] = part[k * per : (k + 1) * per, :].astype(BF16)


def k_cross(scale, where, adjoint, cent_hbm, cross, turned, cent, sem):
    copy = pltpu.make_async_copy(cent_hbm, cent, sem)
    copy.start()
    turned[...] = adjoint[...].T
    copy.wait()
    width = cross.shape[2]
    for k in range(cross.shape[0]):
        block = cent[:, pl.ds(pl.multiple_of(where[k] * width, L), width)]
        part = scale * lax.dot_general(turned[...], block, NN, preferred_element_type=F32)
        cross[k] = part.astype(cross.dtype)


def k_pair(scale, where, turned, cent_hbm, cross_hbm, first, *refs):
    rest, (cent, cross, sems) = refs[:-3], refs[-3:]
    copies = [
        pltpu.make_async_copy(cent_hbm, cent, sems.at[0]),
        pltpu.make_async_copy(cross_hbm, cross, sems.at[1]),
    ]
    for c in copies:
        c.start()
    for c in copies:
        c.wait()
    width = first.shape[1]
    for k, out in enumerate((first, *rest)):
        block = cent[:, pl.ds(pl.multiple_of(where[k] * width, L), width)]
        part = scale * lax.dot_general(turned[...], block, NN, preferred_element_type=F32)
        out[...] = (part + cross[k].astype(F32)).astype(out.dtype)


def k_add(first, *refs):
    value = first[...]
    for r in refs[:-1]:
        value = value + r[...].astype(F32)
    refs[-1][...] = value.astype(BF16).reshape(refs[-1].shape)


def k_sum(recv, out):
    value = recv[0].astype(F32)
    for k in range(1, recv.shape[0]):
        value = value + recv[k].astype(F32)
    out[...] = value.astype(BF16)


def call(body, outs, *args, limit=SMALL, scalars=0, flops=0, hbm_in=(), alias=None, scratch=()):
    spec, far = pl.BlockSpec(memory_space=pltpu.VMEM), pl.BlockSpec(memory_space=pltpu.HBM)
    smem = pl.BlockSpec(memory_space=pltpu.SMEM)
    ins = [smem if i < scalars else far if i in hbm_in else spec for i in range(len(args))]
    size = sum(a.size * a.dtype.itemsize for a in args)
    return pl.pallas_call(
        body,
        out_shape=[jax.ShapeDtypeStruct(s, d) for s, d in outs],
        in_specs=ins,
        out_specs=[spec] * len(outs),
        input_output_aliases=alias or {},
        scratch_shapes=list(scratch),
        compiler_params=pltpu.CompilerParams(vmem_limit_bytes=limit),
        cost_estimate=pl.CostEstimate(flops=flops, bytes_accessed=size, transcendentals=0),
    )(*args)


def shift(value, axis, step):
    n = lax.axis_size(axis)
    return lax.ppermute(value, axis, [(i, (i + step) % n) for i in range(n)])


def shards(embeddings, centroids, plan_grad):
    rows, width = embeddings.shape
    cols, depth = centroids.shape
    ny, nx, nz = lax.axis_size("y"), lax.axis_size("x"), lax.axis_size("z")
    nclus, nprog = ny * 2, nz * nx
    scale = 1.0 / (0.25 * float(depth) ** 0.5)
    ratio = (rows * nprog) / (cols * nclus)
    log_b = math.log(ratio)
    rv, cv = (rows // L, L), (cols // L, L)
    ix, iy, ic = lax.axis_index("x"), lax.axis_index("y"), lax.axis_index("core")

    mine = [embeddings] + [shift(embeddings, "y", k) for k in range(1, ny)]
    theirs = [shift(m, "core", 1) for m in mine]
    source = [lax.rem(iy - k + ny, ny) * 2 for k in range(ny)]
    where = jnp.stack([s + ic for s in source] + [s + 1 - ic for s in source]).astype(jnp.int32)
    (grad,) = call(k_prepare, [((cols, rows), BF16)], plan_grad)
    mine[0], grad = lax.optimization_barrier((mine[0], grad))

    def over_clus(send):
        return lax.all_to_all(send, ("y", "core"), 0, 0, tiled=True)

    def over_prog(send):
        return lax.all_to_all(send, ("z", "x"), 0, 0, tiled=True)

    block = ((cols, rows), F32)
    row_send, col_send = ((nclus, *rv), F32), ((nprog, *cv), F32)
    row_pair, col_pair = ((nclus, 2, *rv), F32), ((nprog, 2, *cv), F32)
    a_row, a_col = (rv, F32), (cv, F32)

    pieces = [*mine, *theirs]
    logits, send = call(
        functools.partial(k_logits, scale),
        [block, row_pair],
        where, centroids, *pieces,
        limit=LARGE, scalars=1, flops=2 * rows * cols * depth,
        hbm_in=range(2, 2 + len(pieces)),
        scratch=[pltpu.VMEM((rows, depth), BF16), pltpu.SemaphoreType.DMA((len(pieces),))],
    )
    row_pot, send = call(k_first_col, [a_row, col_pair], logits, over_clus(send))
    col_pot, weights, send = call(
        functools.partial(k_weights, log_b), [a_col, block, row_send], logits, row_pot, over_prog(send)
    )
    row_mul, col_mul = [], []
    for step in range(1, ITERS):
        recv = over_clus(send)
        if step < ITERS - 1:
            a, send = call(k_col, [a_row, col_send], weights, recv)
            b, send = call(
                functools.partial(k_row, ratio), [a_col, row_send], weights, over_prog(send)
            )
            col_mul.append(b)
        else:
            a, send = call(k_last_col, [a_row, col_pair], weights, grad, recv)
        row_mul.append(a)
    b, x, send = call(
        functools.partial(k_adj_row, ratio),
        [a_col, a_col, row_send],
        weights, grad, over_prog(send),
    )
    col_mul.append(b)
    col_adj, row_adj = [x], []
    for step in range(ITERS - 1, 0, -1):
        y, send = call(
            functools.partial(k_back_col, 1.0 if step == ITERS - 1 else -1.0),
            [a_row, col_send],
            weights, row_mul[step - 1], over_clus(send),
        )
        row_adj.insert(0, y)
        b = col_mul[step - 2] if step > 1 else jnp.ones(cv, F32)
        x, send = call(
            functools.partial(k_back_row, ratio), [a_col, row_send], weights, b, over_prog(send)
        )
        col_adj.insert(0, x)

    target = [lax.rem(iy + k, ny) * 2 for k in range(ny)]
    here = jnp.stack([s + ic for s in target]).astype(jnp.int32)
    there = jnp.stack([s + 1 - ic for s in target]).astype(jnp.int32)
    order = jnp.stack([lax.rem(ix + k, nx) for k in range(nx)]).astype(jnp.int32)
    work = 2 * rows * cols * depth
    recv = over_clus(send)
    base, first = call(
        k_known,
        [block, ((cols, rows), BF16)],
        weights, grad, col_pot, *row_mul, *col_mul, *col_adj, *row_adj,
        flops=work, alias={0: 0, 1: 1},
    )
    per, n = cols // nx, len(pieces)
    adjoint, near, *parts = call(
        functools.partial(k_adjoint, scale),
        [((cols, rows), BF16), ((per, depth), F32)] + [((per, depth), BF16)] * (nx - 1),
        where, order, base, first, recv, *pieces,
        limit=LARGE, scalars=2, flops=work, hbm_in=range(5, 5 + n),
        scratch=[
            pltpu.VMEM((n, rows, width), BF16),
            pltpu.VMEM((cols, rows), BF16),
            pltpu.SemaphoreType.DMA((n,)),
        ],
    )
    parts = [shift(p, "x", k + 1) for k, p in enumerate(parts)]
    cross, turned = call(
        functools.partial(k_cross, scale),
        [((ny, rows, width), BF16), ((rows, cols), BF16)],
        there, adjoint, centroids,
        limit=LARGE, scalars=1, flops=work // 2, hbm_in=(2,),
        scratch=[pltpu.VMEM((cols, depth), BF16), pltpu.SemaphoreType.DMA],
    )
    cross = shift(cross, "core", 1)
    own, *moved = call(
        functools.partial(k_pair, scale),
        [((rows, width), F32)] + [((rows, width), BF16)] * (ny - 1),
        here, turned, centroids, cross,
        limit=LARGE, scalars=1, flops=work // 2, hbm_in=(2, 3),
        scratch=[
            pltpu.VMEM((cols, depth), BF16),
            pltpu.VMEM((ny, rows, width), BF16),
            pltpu.SemaphoreType.DMA((2,)),
        ],
    )
    near, own = lax.optimization_barrier((near, own))
    moved = [shift(m, "y", k + 1) for k, m in enumerate(moved)]
    (parts,) = call(k_add, [((nz, per // nz, depth), BF16)], near, *parts, limit=LARGE)
    parts = lax.all_to_all(parts, "z", 0, 0, tiled=True)
    (centroid_grad,) = call(k_sum, [((per // nz, depth), BF16)], parts, limit=LARGE)
    (embed_grad,) = call(k_add, [((rows, width), BF16)], own, *moved, limit=LARGE)
    return embed_grad, centroid_grad


def solution(mesh):
    shape = dict(mesh.shape)
    nx = 4 if shape["prog"] % 4 == 0 and shape["prog"] > 4 else 2
    grid = (shape["prog"] // nx, nx, shape["clus"] // 2, 2)
    fine = Mesh(mesh.devices.reshape(grid), ("z", "x", "y", "core"))
    prog, clus = ("z", "x"), ("y", "core")
    return jax.shard_map(
        shards,
        mesh=fine,
        in_specs=(P(prog, clus), P(clus, None), P(prog, clus)),
        out_specs=(P(prog, clus), P(clus + prog, None)),
        check_vma=False,
    )
```

```python
import functools
import math

import jax
import jax.numpy as jnp
from jax import lax
from jax.experimental import pallas as pl
from jax.experimental.pallas import tpu as pltpu
from jax.sharding import Mesh
from jax.sharding import PartitionSpec as P


ITERS = 4
L = 128
F32 = jnp.float32
BF16 = jnp.bfloat16
NT = (((1,), (1,)), ((), ()))
NN = (((1,), (0,)), ((), ()))
SMALL = 12 << 20
LARGE = 40 << 20


def spread(vec):
    parts = [jnp.broadcast_to(vec[q : q + 1, :], (L, L)).T for q in range(vec.shape[0])]
    return jnp.concatenate(parts, axis=0)


def put_rows(out, parts):
    whole = jnp.concatenate(parts, axis=0)
    out[...] = jnp.broadcast_to(whole[None], out.shape)


def row_sums(values):
    return [jnp.sum(v, axis=0, keepdims=True) for v in values]


def gather_cols(part):
    return jnp.concatenate(
        [
            jnp.sum(part[q * L : (q + 1) * L, :].T, axis=0, keepdims=True)
            for q in range(part.shape[0] // L)
        ],
        axis=0,
    )


def first_lane(part):
    return jnp.concatenate(
        [part[q * L : (q + 1) * L, :].T[0:1, :] for q in range(part.shape[0] // L)], axis=0
    )


def lanes(ref, r):
    return ref[:, r * L : (r + 1) * L]


def total(recv):
    return jnp.sum(recv[...], axis=0)


def merge(recv):
    tops = recv[:, 0]
    top = jnp.max(tops, axis=0)
    return top + jnp.log(jnp.sum(recv[:, 1] * jnp.exp(tops - top[None]), axis=0))


def k_prepare(plan_grad, grad):
    grad[...] = plan_grad[...].T


def source(ny, k):
    core = lax.axis_index("core") if k < ny else 1 - lax.axis_index("core")
    return lax.rem(lax.axis_index("y") + (ny - k % ny), ny) * 2 + core


def target(ny, k, cross):
    core = 1 - lax.axis_index("core") if cross else lax.axis_index("core")
    return lax.rem(lax.axis_index("y") + k, ny) * 2 + core


def span(at, width):
    return pl.ds(pl.multiple_of(at * width, L), width)


def k_logits(scale, cent, *refs):
    n = len(refs) - 3
    pieces, (logits, send, held) = refs[:n], refs[n:]
    for k, piece in enumerate(pieces):
        held[:, span(source(n // 2, k), piece.shape[1])] = piece[...]
    logits[...] = scale * lax.dot_general(cent[...], held[...], NT, preferred_element_type=F32)
    count = logits.shape[1] // L
    tops, sums = [], []
    for r in range(count):
        tile = lanes(logits, r)
        top = jnp.max(tile, axis=0, keepdims=True)
        tops.append(top)
        sums.append(jnp.sum(jnp.exp(tile - top), axis=0, keepdims=True))
    send[:, 0] = jnp.broadcast_to(jnp.concatenate(tops, axis=0)[None], send[:, 0].shape)
    send[:, 1] = jnp.broadcast_to(jnp.concatenate(sums, axis=0)[None], send[:, 1].shape)


def k_first_col(logits, recv, row_pot, send):
    u = -merge(recv)
    row_pot[...] = u
    count = u.shape[0]
    top = lanes(logits, 0) + u[0:1, :]
    for r in range(1, count):
        top = jnp.maximum(top, lanes(logits, r) + u[r : r + 1, :])
    top = jnp.broadcast_to(jnp.max(top, axis=1, keepdims=True), top.shape)
    part = jnp.exp(lanes(logits, 0) + u[0:1, :] - top)
    for r in range(1, count):
        part = part + jnp.exp(lanes(logits, r) + u[r : r + 1, :] - top)
    send[:, 0] = jnp.broadcast_to(first_lane(top)[None], send[:, 0].shape)
    send[:, 1] = jnp.broadcast_to(gather_cols(part)[None], send[:, 1].shape)


def k_weights(log_b, logits, row_pot, recv, col_pot, weights, send):
    v = log_b - merge(recv)
    col_pot[...] = v
    vv = spread(v)
    u = row_pot[...]
    out = []
    for r in range(u.shape[0]):
        tile = jnp.exp(lanes(logits, r) + u[r : r + 1, :] + vv)
        weights[:, r * L : (r + 1) * L] = tile
        out.append(jnp.sum(tile, axis=0, keepdims=True))
    put_rows(send, out)


def weighted(weights, vec):
    part = lanes(weights, 0) * vec[0:1, :]
    for r in range(1, vec.shape[0]):
        part = part + lanes(weights, r) * vec[r : r + 1, :]
    return part


def k_col(weights, recv, row_mul, send):
    a = 1.0 / total(recv)
    row_mul[...] = a
    send[...] = jnp.broadcast_to(gather_cols(weighted(weights, a))[None], send.shape)


def k_row(ratio, weights, recv, col_mul, send):
    b = ratio / total(recv)
    col_mul[...] = b
    bb = spread(b)
    count = weights.shape[1] // L
    put_rows(send, row_sums([lanes(weights, r) * bb for r in range(count)]))


def k_last_col(weights, grad, recv, row_mul, send):
    a = 1.0 / total(recv)
    row_mul[...] = a
    part = lanes(weights, 0) * a[0:1, :]
    bar = part * lanes(grad, 0).astype(F32)
    for r in range(1, a.shape[0]):
        step = lanes(weights, r) * a[r : r + 1, :]
        part = part + step
        bar = bar + step * lanes(grad, r).astype(F32)
    send[:, 0] = jnp.broadcast_to(gather_cols(part)[None], send[:, 0].shape)
    send[:, 1] = jnp.broadcast_to(gather_cols(bar)[None], send[:, 1].shape)


def k_adj_row(ratio, weights, grad, recv, col_mul, col_adj, send):
    sums = total(recv)
    b = ratio / sums[0]
    x = b * (b * sums[1]) / ratio
    col_mul[...] = b
    col_adj[...] = x
    bb, xx = spread(b), spread(x)
    count = weights.shape[1] // L
    put_rows(
        send,
        row_sums(
            [lanes(weights, r) * (bb * lanes(grad, r).astype(F32) - xx) for r in range(count)]
        ),
    )


def k_back_col(sign, weights, row_mul, recv, row_adj, send):
    a = row_mul[...]
    y = sign * a * a * total(recv)
    row_adj[...] = y
    send[...] = jnp.broadcast_to(gather_cols(weighted(weights, y))[None], send.shape)


def k_back_row(ratio, weights, *refs):
    *col_mul, recv, col_adj, send = refs
    x = total(recv) / -ratio
    for b in col_mul:
        x = x * b[...] * b[...]
    col_adj[...] = x
    xx = spread(x)
    count = weights.shape[1] // L
    put_rows(send, row_sums([lanes(weights, r) * xx for r in range(count)]))


def k_known(weights, grad, col_pot, *refs):
    n = ITERS - 1
    base, first = refs[4 * n + 1 :]
    row_mul = [None] + [r[...] for r in refs[:n]]
    col_mul = [None, None] + [r[...] for r in refs[n : 2 * n]]
    x = [r[...] for r in refs[2 * n : 3 * n + 1]]
    y = [None] + [r[...] for r in refs[3 * n + 1 : 4 * n + 1]]
    b0 = spread(jnp.exp(-col_pot[...]))
    b4 = spread(col_mul[ITERS])
    xs = [spread(v) for v in x]
    bs = [None, None] + [spread(v) for v in col_mul[2:ITERS]]
    for r in range(base.shape[1] // L):
        row = slice(r, r + 1)
        tile = lanes(weights, r)
        inner = (b4 * row_mul[n][row, :]) * lanes(grad, r).astype(F32) - xs[0] - y[1][row, :]
        for t in range(1, ITERS):
            inner = inner - xs[t] * row_mul[t][row, :]
        for t in range(2, ITERS):
            inner = inner - bs[t] * y[t][row, :]
        first[:, r * L : (r + 1) * L] = (tile * b0).astype(BF16)
        base[:, r * L : (r + 1) * L] = tile * inner


def k_adjoint(scale, n, nx, base, first, recv, *refs):
    pieces, adjoint, keep = refs[:n], refs[n], refs[n + 1]
    sends, (held, turned, stage, sems, out_sems) = refs[n + 2 : n + 1 + nx], refs[n + 1 + nx :]
    copies = [
        pltpu.make_async_copy(piece, held.at[k], sems.at[k]) for k, piece in enumerate(pieces)
    ]
    for c in copies:
        c.start()
    y = -total(recv)
    for r in range(y.shape[0]):
        adjoint[:, r * L : (r + 1) * L] = (
            lanes(base, r) - lanes(first, r).astype(F32) * y[r : r + 1, :]
        ).astype(BF16)
    per = keep.shape[0]
    group = 16
    for k in range(nx):
        to = lax.rem(lax.axis_index("x") + k, nx)
        for iz in range(per // group):
            at = pl.multiple_of((iz * nx + to) * group, group)
            turned[k * per + iz * group : k * per + (iz + 1) * group, :] = adjoint[pl.ds(at, group), :]
    width = held.shape[2]
    outs = []
    for p in range(n):
        copies[p].wait()
        part = scale * lax.dot_general(turned[...], held[p], NN, preferred_element_type=F32)
        cols = span(source(n // 2, p), width)
        keep[:, cols] = part[:per, :]
        for k in range(1, nx):
            stage[p, k - 1] = part[k * per : (k + 1) * per, :].astype(BF16)
            outs.append(
                pltpu.make_async_copy(
                    stage.at[p, k - 1], sends[k - 1].at[:, cols], out_sems.at[p, k - 1]
                )
            )
            outs[-1].start()
    for c in outs:
        c.wait()


def k_cross(scale, adjoint, cent, cross, turned, stage, sems):
    turned[...] = adjoint[...].T
    ny, _, width = cross.shape
    outs = []
    for k in range(ny):
        block = cent[:, span(target(ny, k, True), width)]
        part = scale * lax.dot_general(turned[...], block, NN, preferred_element_type=F32)
        stage[k] = part.astype(cross.dtype)
        outs.append(pltpu.make_async_copy(stage.at[k], cross.at[k], sems.at[k]))
        outs[-1].start()
    for c in outs:
        c.wait()


def k_pair(scale, turned, cent, cross, first, *refs):
    rest, (stage, sems) = refs[:-2], refs[-2:]
    ny, _, width = cross.shape
    outs = []
    for k in range(ny - 1, -1, -1):
        block = cent[:, span(target(ny, k, False), width)]
        part = scale * lax.dot_general(turned[...], block, NN, preferred_element_type=F32)
        part = part + cross[k].astype(F32)
        if k:
            stage[k - 1] = part.astype(BF16)
            outs.append(pltpu.make_async_copy(stage.at[k - 1], rest[k - 1], sems.at[k - 1]))
            outs[-1].start()
        else:
            first[...] = part
    for c in outs:
        c.wait()


def k_add(first, *refs):
    value = first[...]
    for r in refs[:-1]:
        value = value + r[...].astype(F32)
    refs[-1][...] = value.astype(BF16).reshape(refs[-1].shape)


def k_sum(recv, out):
    value = recv[0].astype(F32)
    for k in range(1, recv.shape[0]):
        value = value + recv[k].astype(F32)
    out[...] = value.astype(BF16)


def call(body, outs, *args, limit=SMALL, flops=0, hbm_in=(), hbm_out=(), alias=None, scratch=()):
    spec, far = pl.BlockSpec(memory_space=pltpu.VMEM), pl.BlockSpec(memory_space=pltpu.HBM)
    ins = [far if i in hbm_in else spec for i in range(len(args))]
    size = sum(a.size * a.dtype.itemsize for a in args)
    return pl.pallas_call(
        body,
        out_shape=[jax.ShapeDtypeStruct(s, d) for s, d in outs],
        in_specs=ins,
        out_specs=[far if i in hbm_out else spec for i in range(len(outs))],
        input_output_aliases=alias or {},
        scratch_shapes=list(scratch),
        compiler_params=pltpu.CompilerParams(vmem_limit_bytes=limit),
        cost_estimate=pl.CostEstimate(flops=flops, bytes_accessed=size, transcendentals=0),
    )(*args)


def shift(value, axis, step):
    n = lax.axis_size(axis)
    return lax.ppermute(value, axis, [(i, (i + step) % n) for i in range(n)])


def shards(embeddings, centroids, plan_grad):
    rows, width = embeddings.shape
    cols, depth = centroids.shape
    ny, nx, nz = lax.axis_size("y"), lax.axis_size("x"), lax.axis_size("z")
    nclus, nprog = ny * 2, nz * nx
    scale = 1.0 / (0.25 * float(depth) ** 0.5)
    ratio = (rows * nprog) / (cols * nclus)
    log_b = math.log(ratio)
    rv, cv = (rows // L, L), (cols // L, L)

    mine = [embeddings] + [shift(embeddings, "y", k) for k in range(1, ny)]
    theirs = [shift(m, "core", 1) for m in mine]
    (grad,) = call(k_prepare, [((cols, rows), BF16)], plan_grad)
    mine[0], grad = lax.optimization_barrier((mine[0], grad))
    pieces = [*mine, *theirs]

    def over_clus(send):
        return lax.all_to_all(send, ("y", "core"), 0, 0, tiled=True)

    def over_prog(send):
        return lax.all_to_all(send, ("z", "x"), 0, 0, tiled=True)

    block = ((cols, rows), F32)
    row_send, col_send = ((nclus, *rv), F32), ((nprog, *cv), F32)
    row_pair, col_pair = ((nclus, 2, *rv), F32), ((nprog, 2, *cv), F32)
    a_row, a_col = (rv, F32), (cv, F32)

    work = 2 * rows * cols * depth
    logits, send = call(
        functools.partial(k_logits, scale),
        [block, row_pair],
        centroids, *pieces,
        limit=LARGE, flops=work,
        scratch=[pltpu.VMEM((rows, depth), BF16)],
    )
    row_pot, send = call(k_first_col, [a_row, col_pair], logits, over_clus(send))
    col_pot, weights, send = call(
        functools.partial(k_weights, log_b), [a_col, block, row_send], logits, row_pot, over_prog(send)
    )
    row_mul, col_mul = [], []
    for step in range(1, ITERS):
        recv = over_clus(send)
        if step < ITERS - 1:
            a, send = call(k_col, [a_row, col_send], weights, recv)
            b, send = call(
                functools.partial(k_row, ratio), [a_col, row_send], weights, over_prog(send)
            )
            col_mul.append(b)
        else:
            a, send = call(k_last_col, [a_row, col_pair], weights, grad, recv)
        row_mul.append(a)
    b, x, send = call(
        functools.partial(k_adj_row, ratio),
        [a_col, a_col, row_send],
        weights, grad, over_prog(send),
    )
    col_mul.append(b)
    col_adj, row_adj = [x], []
    for step in range(ITERS - 1, 0, -1):
        y, send = call(
            functools.partial(k_back_col, 1.0 if step == ITERS - 1 else -1.0),
            [a_row, col_send],
            weights, row_mul[step - 1], over_clus(send),
        )
        row_adj.insert(0, y)
        b = col_mul[step - 2 : step - 1] if step > 1 else []
        x, send = call(
            functools.partial(k_back_row, ratio), [a_col, row_send], weights, *b, over_prog(send)
        )
        col_adj.insert(0, x)

    recv = over_clus(send)
    base, first = call(
        k_known,
        [block, ((cols, rows), BF16)],
        weights, grad, col_pot, *row_mul, *col_mul, *col_adj, *row_adj,
        flops=work, alias={0: 0, 1: 1},
    )
    per, n = cols // nx, len(pieces)
    adjoint, near, *parts = call(
        functools.partial(k_adjoint, scale, n, nx),
        [((cols, rows), BF16), ((per, depth), F32)] + [((per, depth), BF16)] * (nx - 1),
        base, first, recv,
        *(pltpu.with_memory_space_constraint(p, pltpu.HBM) for p in pieces),
        limit=LARGE, flops=work, hbm_in=range(3, 3 + n), hbm_out=range(2, 1 + nx),
        scratch=[
            pltpu.VMEM((n, rows, width), BF16),
            pltpu.VMEM((cols, rows), BF16),
            pltpu.VMEM((n, nx - 1, per, width), BF16),
            pltpu.SemaphoreType.DMA((n,)),
            pltpu.SemaphoreType.DMA((n, nx - 1)),
        ],
    )
    parts = [shift(p, "x", k + 1) for k, p in enumerate(parts)]
    cross, turned = call(
        functools.partial(k_cross, scale),
        [((ny, rows, width), BF16), ((rows, cols), BF16)],
        adjoint, centroids,
        limit=LARGE, flops=work // 2, hbm_out=(0,),
        scratch=[pltpu.VMEM((ny, rows, width), BF16), pltpu.SemaphoreType.DMA((ny,))],
    )
    cross = shift(cross, "core", 1)
    own, *moved = call(
        functools.partial(k_pair, scale),
        [((rows, width), F32)] + [((rows, width), BF16)] * (ny - 1),
        turned, centroids, cross,
        limit=LARGE, flops=work // 2, hbm_out=range(1, ny),
        scratch=[pltpu.VMEM((ny - 1, rows, width), BF16), pltpu.SemaphoreType.DMA((ny - 1,))],
    )
    near, own = lax.optimization_barrier((near, own))
    moved = [shift(m, "y", k + 1) for k, m in enumerate(moved)]
    (parts,) = call(k_add, [((nz, per // nz, depth), BF16)], near, *parts, limit=LARGE)
    parts = lax.all_to_all(parts, "z", 0, 0, tiled=True)
    (centroid_grad,) = call(k_sum, [((per // nz, depth), BF16)], parts, limit=LARGE)
    (embed_grad,) = call(k_add, [((rows, width), BF16)], own, *moved, limit=LARGE)
    return embed_grad, centroid_grad


def solution(mesh):
    shape = dict(mesh.shape)
    nx = 4 if shape["prog"] % 4 == 0 and shape["prog"] > 4 else 2
    grid = (shape["prog"] // nx, nx, shape["clus"] // 2, 2)
    fine = Mesh(mesh.devices.reshape(grid), ("z", "x", "y", "core"))
    prog, clus = ("z", "x"), ("y", "core")
    return jax.shard_map(
        shards,
        mesh=fine,
        in_specs=(P(prog, clus), P(clus, None), P(prog, clus)),
        out_specs=(P(prog, clus), P(clus + prog, None)),
        check_vma=False,
    )
```

```python
import functools
import math

import jax
import jax.numpy as jnp
from jax import lax
from jax.experimental import pallas as pl
from jax.experimental.pallas import tpu as pltpu
from jax.sharding import Mesh
from jax.sharding import PartitionSpec as P


ITERS = 4
L = 128
F32 = jnp.float32
BF16 = jnp.bfloat16
NT = (((1,), (1,)), ((), ()))
NN = (((1,), (0,)), ((), ()))
SMALL = 12 << 20
LARGE = 40 << 20


def spread(vec):
    parts = [jnp.broadcast_to(vec[q : q + 1, :], (L, L)).T for q in range(vec.shape[0])]
    return jnp.concatenate(parts, axis=0)


def put_rows(out, parts):
    whole = jnp.concatenate(parts, axis=0)
    out[...] = jnp.broadcast_to(whole[None], out.shape)


def row_sums(values):
    return [jnp.sum(v, axis=0, keepdims=True) for v in values]


def gather_cols(part):
    return jnp.concatenate(
        [
            jnp.sum(part[q * L : (q + 1) * L, :].T, axis=0, keepdims=True)
            for q in range(part.shape[0] // L)
        ],
        axis=0,
    )


def first_lane(part):
    return jnp.concatenate(
        [part[q * L : (q + 1) * L, :].T[0:1, :] for q in range(part.shape[0] // L)], axis=0
    )


def lanes(ref, r):
    return ref[:, r * L : (r + 1) * L]


def total(recv):
    return jnp.sum(recv[...].astype(F32), axis=0)


def put_cols(out, part):
    out[...] = jnp.broadcast_to(gather_cols(part)[None], out.shape).astype(out.dtype)


def merge(recv):
    tops = recv[:, 0]
    top = jnp.max(tops, axis=0)
    return top + jnp.log(jnp.sum(recv[:, 1] * jnp.exp(tops - top[None]), axis=0))


def k_prepare(plan_grad, grad):
    grad[...] = plan_grad[...].T


def source(ny, k):
    core = lax.axis_index("core") if k < ny else 1 - lax.axis_index("core")
    return lax.rem(lax.axis_index("y") + (ny - k % ny), ny) * 2 + core


def target(ny, k, cross):
    core = 1 - lax.axis_index("core") if cross else lax.axis_index("core")
    return lax.rem(lax.axis_index("y") + k, ny) * 2 + core


def by_z():
    return (0,)


def by_x(n):
    return tuple(k for k in range(n) if k not in by_z())


def span(at, width):
    return pl.ds(pl.multiple_of(at * width, L), width)


def k_logits(scale, cent, *refs):
    n = len(refs) - 3
    pieces, (logits, send, held) = refs[:n], refs[n:]
    for k, piece in enumerate(pieces):
        held[:, span(source(n // 2, k), piece.shape[1])] = piece[...]
    logits[...] = scale * lax.dot_general(cent[...], held[...], NT, preferred_element_type=F32)
    count = logits.shape[1] // L
    tops, sums = [], []
    for r in range(count):
        tile = lanes(logits, r)
        top = jnp.max(tile, axis=0, keepdims=True)
        tops.append(top)
        sums.append(jnp.sum(jnp.exp(tile - top), axis=0, keepdims=True))
    send[:, 0] = jnp.broadcast_to(jnp.concatenate(tops, axis=0)[None], send[:, 0].shape)
    send[:, 1] = jnp.broadcast_to(jnp.concatenate(sums, axis=0)[None], send[:, 1].shape)


def k_first_col(logits, recv, row_pot, send):
    u = -merge(recv)
    row_pot[...] = u
    count = u.shape[0]
    top = lanes(logits, 0) + u[0:1, :]
    for r in range(1, count):
        top = jnp.maximum(top, lanes(logits, r) + u[r : r + 1, :])
    top = jnp.broadcast_to(jnp.max(top, axis=1, keepdims=True), top.shape)
    part = jnp.exp(lanes(logits, 0) + u[0:1, :] - top)
    for r in range(1, count):
        part = part + jnp.exp(lanes(logits, r) + u[r : r + 1, :] - top)
    send[:, 0] = jnp.broadcast_to(first_lane(top)[None], send[:, 0].shape)
    send[:, 1] = jnp.broadcast_to(gather_cols(part)[None], send[:, 1].shape)


def k_weights(log_b, logits, row_pot, recv, col_pot, weights, send):
    v = log_b - merge(recv)
    col_pot[...] = v
    vv = spread(v)
    u = row_pot[...]
    out = []
    for r in range(u.shape[0]):
        tile = jnp.exp(lanes(logits, r) + u[r : r + 1, :] + vv)
        weights[:, r * L : (r + 1) * L] = tile
        out.append(jnp.sum(tile, axis=0, keepdims=True))
    put_rows(send, out)


def weighted(weights, vec):
    part = lanes(weights, 0) * vec[0:1, :]
    for r in range(1, vec.shape[0]):
        part = part + lanes(weights, r) * vec[r : r + 1, :]
    return part


def k_col(weights, recv, row_mul, send):
    a = 1.0 / total(recv)
    row_mul[...] = a
    put_cols(send, weighted(weights, a))


def k_row(ratio, weights, recv, col_mul, send):
    b = ratio / total(recv)
    col_mul[...] = b
    bb = spread(b)
    count = weights.shape[1] // L
    put_rows(send, row_sums([lanes(weights, r) * bb for r in range(count)]))


def k_last_col(weights, grad, recv, row_mul, send):
    a = 1.0 / total(recv)
    row_mul[...] = a
    part = lanes(weights, 0) * a[0:1, :]
    bar = part * lanes(grad, 0).astype(F32)
    for r in range(1, a.shape[0]):
        step = lanes(weights, r) * a[r : r + 1, :]
        part = part + step
        bar = bar + step * lanes(grad, r).astype(F32)
    both = jnp.stack([gather_cols(part), gather_cols(bar)])
    send[...] = jnp.broadcast_to(both[None], send.shape).astype(send.dtype)


def k_adj_row(ratio, weights, grad, recv, col_mul, col_adj, send):
    sums = total(recv)
    b = ratio / sums[0]
    x = b * (b * sums[1]) / ratio
    col_mul[...] = b
    col_adj[...] = x
    bb, xx = spread(b), spread(x)
    count = weights.shape[1] // L
    put_rows(
        send,
        row_sums(
            [lanes(weights, r) * (bb * lanes(grad, r).astype(F32) - xx) for r in range(count)]
        ),
    )


def k_back_col(sign, weights, row_mul, recv, row_adj, send):
    a = row_mul[...]
    y = sign * a * a * total(recv)
    row_adj[...] = y
    put_cols(send, weighted(weights, y))


def k_back_row(ratio, weights, *refs):
    *col_mul, recv, col_adj, send = refs
    x = total(recv) / -ratio
    for b in col_mul:
        x = x * b[...] * b[...]
    col_adj[...] = x
    xx = spread(x)
    count = weights.shape[1] // L
    put_rows(send, row_sums([lanes(weights, r) * xx for r in range(count)]))


def k_known(weights, grad, col_pot, *refs):
    n = ITERS - 1
    base, first = refs[4 * n + 1 :]
    row_mul = [None] + [r[...] for r in refs[:n]]
    col_mul = [None, None] + [r[...] for r in refs[n : 2 * n]]
    x = [r[...] for r in refs[2 * n : 3 * n + 1]]
    y = [None] + [r[...] for r in refs[3 * n + 1 : 4 * n + 1]]
    b0 = spread(jnp.exp(-col_pot[...]))
    b4 = spread(col_mul[ITERS])
    xs = [spread(v) for v in x]
    bs = [None, None] + [spread(v) for v in col_mul[2:ITERS]]
    for r in range(base.shape[1] // L):
        row = slice(r, r + 1)
        tile = lanes(weights, r)
        inner = (b4 * row_mul[n][row, :]) * lanes(grad, r).astype(F32) - xs[0] - y[1][row, :]
        for t in range(1, ITERS):
            inner = inner - xs[t] * row_mul[t][row, :]
        for t in range(2, ITERS):
            inner = inner - bs[t] * y[t][row, :]
        first[:, r * L : (r + 1) * L] = (tile * b0).astype(BF16)
        base[:, r * L : (r + 1) * L] = tile * inner


def k_adjoint(scale, base, first, recv, cent_hbm, adjoint, turned_hbm, cross, cent, turned, sems):
    copy = pltpu.make_async_copy(cent_hbm, cent, sems.at[0])
    copy.start()
    y = -total(recv)
    for r in range(y.shape[0]):
        tile = lanes(base, r) - lanes(first, r).astype(F32) * y[r : r + 1, :]
        tile = tile.astype(BF16)
        adjoint[:, r * L : (r + 1) * L] = tile
        turned[r * L : (r + 1) * L, :] = tile.T
    back = pltpu.make_async_copy(turned, turned_hbm, sems.at[1])
    back.start()
    copy.wait()
    ny, _, width = cross.shape
    for k in range(ny):
        block = cent[:, span(target(ny, k, True), width)]
        part = scale * lax.dot_general(turned[...], block, NN, preferred_element_type=F32)
        cross[k] = part.astype(BF16)
    back.wait()


def k_cent(scale, n, nx, adjoint, *refs):
    pieces, straight, keep = refs[:n], refs[n], refs[n + 1]
    sends, (picked, wide, own, narrow, sems) = refs[n + 2 : n + 1 + nx], refs[n + 1 + nx :]
    per = keep.shape[0]
    group = 16
    for k in range(nx):
        to = lax.rem(lax.axis_index("x") + k, nx)
        for iz in range(per // group):
            at = pl.multiple_of((iz * nx + to) * group, group)
            picked[k * per + iz * group : k * per + (iz + 1) * group, :] = adjoint[pl.ds(at, group), :]
    width = pieces[0].shape[1]
    outs = []

    def leave(src, dst):
        outs.append(pltpu.make_async_copy(src, dst, sems.at[len(outs)]))
        outs[-1].start()

    for i, p in enumerate(by_z()):
        part = scale * lax.dot_general(adjoint[...], pieces[p][...], NN, preferred_element_type=F32)
        narrow[i] = part.astype(BF16).reshape(narrow.shape[1:])
        leave(narrow.at[i], straight.at[:, :, pl.ds(i * width, width)])
    for i, p in enumerate(by_x(n)):
        part = scale * lax.dot_general(picked[...], pieces[p][...], NN, preferred_element_type=F32)
        own[i] = part[:per, :]
        leave(own.at[i], keep.at[:, pl.ds(i * width, width)])
        for k in range(1, nx):
            wide[i, k - 1] = part[k * per : (k + 1) * per, :].astype(BF16)
            leave(wide.at[i, k - 1], sends[k - 1].at[:, pl.ds(i * width, width)])
    for c in outs:
        c.wait()


def k_pair(scale, turned, cent, cross, first, *rest):
    ny, _, width = cross.shape
    for k, out in enumerate((first, *rest)):
        block = cent[:, span(target(ny, k, False), width)]
        part = scale * lax.dot_general(turned[...], block, NN, preferred_element_type=F32)
        out[...] = (part + cross[k].astype(F32)).astype(out.dtype)


def k_early(recv, keep, *refs):
    sends, held = refs[:-1], refs[-1]
    value = recv[0].astype(F32)
    for k in range(1, recv.shape[0]):
        value = value + recv[k].astype(F32)
    held[...] = value
    rows, nx = keep.shape[0], len(sends) + 1
    for k, out in enumerate((keep, *sends)):
        at = lax.rem(lax.axis_index("x") + k, nx) * rows
        out[...] = held[pl.ds(pl.multiple_of(at, 16), rows), :].astype(out.dtype)


def k_join(n, one, keep, *refs):
    out = refs[-1]
    width = out.shape[1] // n
    first = one[0].astype(F32)
    for k in range(1, one.shape[0]):
        first = first + one[k].astype(F32)
    second = keep[...]
    for r in refs[:-1]:
        second = second + r[...].astype(F32)
    for value, pieces in ((first.astype(BF16), by_x(n)), (second.astype(BF16), by_z())):
        for i, p in enumerate(pieces):
            out[:, span(source(n // 2, p), width)] = value[:, i * width : (i + 1) * width]


def k_add(first, *refs):
    value = first[...]
    for r in refs[:-1]:
        value = value + r[...].astype(F32)
    refs[-1][...] = value.astype(BF16).reshape(refs[-1].shape)


def call(body, outs, *args, limit=SMALL, flops=0, hbm_in=(), hbm_out=(), alias=None, scratch=()):
    spec, far = pl.BlockSpec(memory_space=pltpu.VMEM), pl.BlockSpec(memory_space=pltpu.HBM)
    ins = [far if i in hbm_in else spec for i in range(len(args))]
    size = sum(a.size * a.dtype.itemsize for a in args)
    return pl.pallas_call(
        body,
        out_shape=[
            pltpu.HBM(s, d) if i in hbm_out else jax.ShapeDtypeStruct(s, d)
            for i, (s, d) in enumerate(outs)
        ],
        in_specs=ins,
        out_specs=[far if i in hbm_out else spec for i in range(len(outs))],
        input_output_aliases=alias or {},
        scratch_shapes=list(scratch),
        compiler_params=pltpu.CompilerParams(vmem_limit_bytes=limit),
        cost_estimate=pl.CostEstimate(flops=flops, bytes_accessed=size, transcendentals=0),
    )(*args)


def shift(value, axis, step):
    n = lax.axis_size(axis)
    return lax.ppermute(value, axis, [(i, (i + step) % n) for i in range(n)])


def shards(embeddings, centroids, plan_grad):
    rows, width = embeddings.shape
    cols, depth = centroids.shape
    ny, nx, nz = lax.axis_size("y"), lax.axis_size("x"), lax.axis_size("z")
    nclus, nprog = ny * 2, nz * nx
    scale = 1.0 / (0.25 * float(depth) ** 0.5)
    ratio = (rows * nprog) / (cols * nclus)
    log_b = math.log(ratio)
    rv, cv = (rows // L, L), (cols // L, L)

    mine = [embeddings] + [shift(embeddings, "y", k) for k in range(1, ny)]
    theirs = [shift(m, "core", 1) for m in mine]
    (grad,) = call(k_prepare, [((cols, rows), BF16)], plan_grad)
    mine[0], grad = lax.optimization_barrier((mine[0], grad))
    pieces = [*mine, *theirs]

    def over_clus(send):
        return lax.all_to_all(send, ("y", "core"), 0, 0, tiled=True)

    def over_prog(send):
        return lax.all_to_all(send, ("z", "x"), 0, 0, tiled=True)

    block = ((cols, rows), F32)
    row_send, col_send = ((nclus, *rv), F32), ((nprog, *cv), F32)
    row_pair, col_pair = ((nclus, 2, *rv), F32), ((nprog, 2, *cv), F32)
    a_row, a_col = (rv, F32), (cv, F32)

    work = 2 * rows * cols * depth
    logits, send = call(
        functools.partial(k_logits, scale),
        [block, row_pair],
        centroids, *pieces,
        limit=LARGE, flops=work,
        scratch=[pltpu.VMEM((rows, depth), BF16)],
    )
    row_pot, send = call(k_first_col, [a_row, col_pair], logits, over_clus(send))
    col_pot, weights, send = call(
        functools.partial(k_weights, log_b), [a_col, block, row_send], logits, row_pot, over_prog(send)
    )
    row_mul, col_mul = [], []
    for step in range(1, ITERS):
        recv = over_clus(send)
        if step < ITERS - 1:
            a, send = call(k_col, [a_row, col_send], weights, recv)
            b, send = call(
                functools.partial(k_row, ratio), [a_col, row_send], weights, over_prog(send)
            )
            col_mul.append(b)
        else:
            a, send = call(k_last_col, [a_row, col_pair], weights, grad, recv)
        row_mul.append(a)
    b, x, send = call(
        functools.partial(k_adj_row, ratio),
        [a_col, a_col, row_send],
        weights, grad, over_prog(send),
    )
    col_mul.append(b)
    col_adj, row_adj = [x], []
    for step in range(ITERS - 1, 0, -1):
        y, send = call(
            functools.partial(k_back_col, 1.0 if step == ITERS - 1 else -1.0),
            [a_row, col_send],
            weights, row_mul[step - 1], over_clus(send),
        )
        row_adj.insert(0, y)
        b = col_mul[step - 2 : step - 1] if step > 1 else []
        x, send = call(
            functools.partial(k_back_row, ratio), [a_col, row_send], weights, *b, over_prog(send)
        )
        col_adj.insert(0, x)

    recv = over_clus(send)
    base, first = call(
        k_known,
        [block, ((cols, rows), BF16)],
        weights, grad, col_pot, *row_mul, *col_mul, *col_adj, *row_adj,
        flops=work, alias={0: 0, 1: 1},
    )
    per, n = cols // nx, len(pieces)
    adjoint, turned, cross = call(
        functools.partial(k_adjoint, scale),
        [((cols, rows), BF16), ((rows, cols), BF16), ((ny, rows, width), BF16)],
        base, first, recv, pltpu.with_memory_space_constraint(centroids, pltpu.HBM),
        limit=LARGE, flops=work // 2, hbm_in=(3,), hbm_out=(1,),
        scratch=[
            pltpu.VMEM((cols, depth), BF16),
            pltpu.VMEM((rows, cols), BF16),
            pltpu.SemaphoreType.DMA((2,)),
        ],
    )
    cross = shift(cross, "core", 1)
    wide, narrow = len(by_x(n)) * width, len(by_z()) * width
    straight, near, *parts = call(
        functools.partial(k_cent, scale, n, nx),
        [((nz, cols // nz, narrow), BF16), ((per, wide), F32)]
        + [((per, wide), BF16)] * (nx - 1),
        adjoint, *pieces,
        limit=LARGE, flops=work, hbm_out=range(1 + nx),
        scratch=[
            pltpu.VMEM((cols, rows), BF16),
            pltpu.VMEM((len(by_x(n)), nx - 1, per, width), BF16),
            pltpu.VMEM((len(by_x(n)), per, width), F32),
            pltpu.VMEM((len(by_z()), nz, cols // nz, width), BF16),
            pltpu.SemaphoreType.DMA((n * nx,)),
        ],
    )
    parts = [shift(p, "x", k + 1) for k, p in enumerate(parts)]
    straight = lax.all_to_all(straight, "z", 0, 0, tiled=True)
    own, *moved = call(
        functools.partial(k_pair, scale),
        [((rows, width), F32)] + [((rows, width), BF16)] * (ny - 1),
        turned, centroids, cross,
        limit=LARGE, flops=work // 2,
    )
    near, own = lax.optimization_barrier((near, own))
    moved = [shift(m, "y", k + 1) for k, m in enumerate(moved)]
    (parts,) = call(k_add, [((nz, per // nz, wide), BF16)], near, *parts, limit=LARGE)
    parts = lax.all_to_all(parts, "z", 0, 0, tiled=True)
    final = per // nz
    last, *late = call(
        k_early,
        [((final, narrow), F32)] + [((final, narrow), BF16)] * (nx - 1),
        straight,
        limit=LARGE, scratch=[pltpu.VMEM((cols // nz, narrow), F32)],
    )
    late = [shift(p, "x", k + 1) for k, p in enumerate(late)]
    (embed_grad,) = call(k_add, [((rows, width), BF16)], own, *moved, limit=LARGE)
    (centroid_grad,) = call(
        functools.partial(k_join, n), [((final, depth), BF16)], parts, last, *late, limit=LARGE
    )
    return embed_grad, centroid_grad


def solution(mesh):
    shape = dict(mesh.shape)
    nx = 4 if shape["prog"] % 4 == 0 and shape["prog"] > 4 else 2
    grid = (shape["prog"] // nx, nx, shape["clus"] // 2, 2)
    fine = Mesh(mesh.devices.reshape(grid), ("z", "x", "y", "core"))
    prog, clus = ("z", "x"), ("y", "core")
    return jax.shard_map(
        shards,
        mesh=fine,
        in_specs=(P(prog, clus), P(clus, None), P(prog, clus)),
        out_specs=(P(prog, clus), P(clus + prog, None)),
        check_vma=False,
    )
```

```python
import functools
import math

import jax
import jax.numpy as jnp
from jax import lax
from jax.experimental import pallas as pl
from jax.experimental.pallas import tpu as pltpu
from jax.sharding import Mesh
from jax.sharding import PartitionSpec as P


ITERS = 4
L = 128
F32 = jnp.float32
BF16 = jnp.bfloat16
NT = (((1,), (1,)), ((), ()))
NN = (((1,), (0,)), ((), ()))
SMALL = 12 << 20
LARGE = 40 << 20


def spread(vec):
    parts = [jnp.broadcast_to(vec[q : q + 1, :], (L, L)).T for q in range(vec.shape[0])]
    return jnp.concatenate(parts, axis=0)


def put_rows(out, parts):
    whole = jnp.concatenate(parts, axis=0)
    out[...] = jnp.broadcast_to(whole[None], out.shape)


def row_sums(values):
    return [jnp.sum(v, axis=0, keepdims=True) for v in values]


def gather_cols(part):
    return jnp.concatenate(
        [
            jnp.sum(part[q * L : (q + 1) * L, :].T, axis=0, keepdims=True)
            for q in range(part.shape[0] // L)
        ],
        axis=0,
    )


def first_lane(part):
    return jnp.concatenate(
        [part[q * L : (q + 1) * L, :].T[0:1, :] for q in range(part.shape[0] // L)], axis=0
    )


def lanes(ref, r):
    return ref[:, r * L : (r + 1) * L]


def total(recv):
    return jnp.sum(recv[...].astype(F32), axis=0)


def put_cols(out, part):
    out[...] = jnp.broadcast_to(gather_cols(part)[None], out.shape).astype(out.dtype)


def merge(recv):
    tops = recv[:, 0]
    top = jnp.max(tops, axis=0)
    return top + jnp.log(jnp.sum(recv[:, 1] * jnp.exp(tops - top[None]), axis=0))


def k_prepare(plan_grad, grad):
    grad[...] = plan_grad[...].T


def source(ny, k):
    core = lax.axis_index("core") if k < ny else 1 - lax.axis_index("core")
    return lax.rem(lax.axis_index("y") + (ny - k % ny), ny) * 2 + core


def target(ny, k, cross):
    core = 1 - lax.axis_index("core") if cross else lax.axis_index("core")
    return lax.rem(lax.axis_index("y") + k, ny) * 2 + core


def by_z():
    return (0,)


def by_x(n):
    return tuple(k for k in range(n) if k not in by_z())


def span(at, width):
    return pl.ds(pl.multiple_of(at * width, L), width)


def grouped(refs, counts):
    out, at = [], 0
    for c in counts:
        out.append(refs[at : at + c])
        at += c
    return out


def k_logits(scale, counts, cent, *refs):
    n = len(counts)
    pieces, (logits, send, whole, held, sem) = grouped(refs, counts), refs[sum(counts) :]
    for k, blocks in enumerate(pieces):
        at = 0
        for block in blocks:
            rows = slice(at, at + block.shape[0])
            held[rows, span(source(n // 2, k), block.shape[1])] = block[...]
            at += block.shape[0]
    copy = pltpu.make_async_copy(held, whole, sem)
    copy.start()
    logits[...] = scale * lax.dot_general(cent[...], held[...], NT, preferred_element_type=F32)
    count = logits.shape[1] // L
    tops, sums = [], []
    for r in range(count):
        tile = lanes(logits, r)
        top = jnp.max(tile, axis=0, keepdims=True)
        tops.append(top)
        sums.append(jnp.sum(jnp.exp(tile - top), axis=0, keepdims=True))
    send[:, 0] = jnp.broadcast_to(jnp.concatenate(tops, axis=0)[None], send[:, 0].shape)
    send[:, 1] = jnp.broadcast_to(jnp.concatenate(sums, axis=0)[None], send[:, 1].shape)
    copy.wait()


def k_first_col(logits, recv, row_pot, send):
    u = -merge(recv)
    row_pot[...] = u
    count = u.shape[0]
    top = lanes(logits, 0) + u[0:1, :]
    for r in range(1, count):
        top = jnp.maximum(top, lanes(logits, r) + u[r : r + 1, :])
    top = jnp.broadcast_to(jnp.max(top, axis=1, keepdims=True), top.shape)
    part = jnp.exp(lanes(logits, 0) + u[0:1, :] - top)
    for r in range(1, count):
        part = part + jnp.exp(lanes(logits, r) + u[r : r + 1, :] - top)
    send[:, 0] = jnp.broadcast_to(first_lane(top)[None], send[:, 0].shape)
    send[:, 1] = jnp.broadcast_to(gather_cols(part)[None], send[:, 1].shape)


def k_weights(log_b, logits, row_pot, recv, col_pot, weights, send):
    v = log_b - merge(recv)
    col_pot[...] = v
    vv = spread(v)
    u = row_pot[...]
    out = []
    for r in range(u.shape[0]):
        tile = jnp.exp(lanes(logits, r) + u[r : r + 1, :] + vv)
        weights[:, r * L : (r + 1) * L] = tile
        out.append(jnp.sum(tile, axis=0, keepdims=True))
    put_rows(send, out)


def weighted(weights, vec):
    part = lanes(weights, 0) * vec[0:1, :]
    for r in range(1, vec.shape[0]):
        part = part + lanes(weights, r) * vec[r : r + 1, :]
    return part


def k_col(weights, recv, row_mul, send):
    a = 1.0 / total(recv)
    row_mul[...] = a
    put_cols(send, weighted(weights, a))


def k_row(ratio, weights, recv, col_mul, send):
    b = ratio / total(recv)
    col_mul[...] = b
    bb = spread(b)
    count = weights.shape[1] // L
    put_rows(send, row_sums([lanes(weights, r) * bb for r in range(count)]))


def k_last_col(weights, grad, recv, row_mul, send):
    a = 1.0 / total(recv)
    row_mul[...] = a
    part = lanes(weights, 0) * a[0:1, :]
    bar = part * lanes(grad, 0).astype(F32)
    for r in range(1, a.shape[0]):
        step = lanes(weights, r) * a[r : r + 1, :]
        part = part + step
        bar = bar + step * lanes(grad, r).astype(F32)
    both = jnp.stack([gather_cols(part), gather_cols(bar)])
    send[...] = jnp.broadcast_to(both[None], send.shape).astype(send.dtype)


def k_adj_row(ratio, weights, grad, recv, col_mul, col_adj, send):
    sums = total(recv)
    b = ratio / sums[0]
    x = b * (b * sums[1]) / ratio
    col_mul[...] = b
    col_adj[...] = x
    bb, xx = spread(b), spread(x)
    count = weights.shape[1] // L
    put_rows(
        send,
        row_sums(
            [lanes(weights, r) * (bb * lanes(grad, r).astype(F32) - xx) for r in range(count)]
        ),
    )


def k_back_col(sign, weights, row_mul, recv, row_adj, send):
    a = row_mul[...]
    y = sign * a * a * total(recv)
    row_adj[...] = y
    put_cols(send, weighted(weights, y))


def k_back_row(ratio, weights, *refs):
    *col_mul, recv, col_adj, send = refs
    x = total(recv) / -ratio
    for b in col_mul:
        x = x * b[...] * b[...]
    col_adj[...] = x
    xx = spread(x)
    count = weights.shape[1] // L
    put_rows(send, row_sums([lanes(weights, r) * xx for r in range(count)]))


def k_known(weights, grad, col_pot, *refs):
    n = ITERS - 1
    base, first = refs[4 * n + 1 :]
    row_mul = [None] + [r[...] for r in refs[:n]]
    col_mul = [None, None] + [r[...] for r in refs[n : 2 * n]]
    x = [r[...] for r in refs[2 * n : 3 * n + 1]]
    y = [None] + [r[...] for r in refs[3 * n + 1 : 4 * n + 1]]
    b0 = spread(jnp.exp(-col_pot[...]))
    b4 = spread(col_mul[ITERS])
    xs = [spread(v) for v in x]
    bs = [None, None] + [spread(v) for v in col_mul[2:ITERS]]
    for r in range(base.shape[1] // L):
        row = slice(r, r + 1)
        tile = lanes(weights, r)
        inner = (b4 * row_mul[n][row, :]) * lanes(grad, r).astype(F32) - xs[0] - y[1][row, :]
        for t in range(1, ITERS):
            inner = inner - xs[t] * row_mul[t][row, :]
        for t in range(2, ITERS):
            inner = inner - bs[t] * y[t][row, :]
        first[:, r * L : (r + 1) * L] = (tile * b0).astype(BF16)
        base[:, r * L : (r + 1) * L] = tile * inner


def k_adjoint(base, first, recv, adjoint, turned):
    y = -total(recv)
    for r in range(y.shape[0]):
        tile = lanes(base, r) - lanes(first, r).astype(F32) * y[r : r + 1, :]
        tile = tile.astype(BF16)
        adjoint[:, r * L : (r + 1) * L] = tile
        turned[r * L : (r + 1) * L, :] = tile.T


def k_cent(scale, n, nx, adjoint, whole_hbm, straight, keep, *refs):
    sends, (whole, picked, wide, own, narrow, sems, in_sems) = refs[: nx - 1], refs[nx - 1 :]
    width = whole.shape[2]
    copies = [
        pltpu.make_async_copy(
            whole_hbm.at[:, span(source(n // 2, p), width)], whole.at[p], in_sems.at[p]
        )
        for p in range(n)
    ]
    for p in (*by_x(n), *by_z()):
        copies[p].start()
    per = keep.shape[0]
    group = 16
    for k in range(nx):
        to = lax.rem(lax.axis_index("x") + k, nx)
        for iz in range(per // group):
            at = pl.multiple_of((iz * nx + to) * group, group)
            picked[k * per + iz * group : k * per + (iz + 1) * group, :] = adjoint[pl.ds(at, group), :]
    outs = []

    def leave(src, dst):
        outs.append(pltpu.make_async_copy(src, dst, sems.at[len(outs)]))
        outs[-1].start()

    def product(left, p):
        copies[p].wait()
        return scale * lax.dot_general(left[...], whole[p], NN, preferred_element_type=F32)

    for i, p in enumerate(by_x(n)):
        part = product(picked, p)
        for k in range(1, nx):
            wide[i, k - 1] = part[k * per : (k + 1) * per, :].astype(BF16)
            leave(wide.at[i, k - 1], sends[k - 1].at[:, pl.ds(i * width, width)])
        own[i] = part[:per, :]
        leave(own.at[i], keep.at[:, pl.ds(i * width, width)])
    for i, p in enumerate(by_z()):
        part = product(adjoint, p)
        narrow[i] = part.astype(BF16).reshape(narrow.shape[1:])
        leave(narrow.at[i], straight.at[:, :, pl.ds(i * width, width)])
    for c in outs:
        c.wait()


def k_cross(scale, turned, cent, cross_hbm, turned_hbm, cross, sems):
    ny, _, width = cross.shape
    outs = [pltpu.make_async_copy(turned, turned_hbm, sems.at[ny])]
    outs[0].start()
    for k in range(ny):
        block = cent[:, span(target(ny, k, True), width)]
        part = scale * lax.dot_general(turned[...], block, NN, preferred_element_type=F32)
        cross[k] = part.astype(BF16)
        outs.append(pltpu.make_async_copy(cross.at[k], cross_hbm.at[k], sems.at[k]))
        outs[-1].start()
    for c in outs:
        c.wait()


def k_pair(scale, turned_hbm, cent, cross_hbm, first, *refs):
    rest, (turned, cross, own, stage, sems, out_sems) = refs[:-6], refs[-6:]
    ny, _, width = cross.shape
    bring = pltpu.make_async_copy(turned_hbm, turned, sems.at[ny])
    bring.start()
    copies = [
        pltpu.make_async_copy(cross_hbm.at[k], cross.at[k], sems.at[k]) for k in range(ny)
    ]
    for k in range(ny - 1, -1, -1):
        copies[k].start()
    bring.wait()
    outs = []
    for k in range(ny - 1, -1, -1):
        block = cent[:, span(target(ny, k, False), width)]
        part = scale * lax.dot_general(turned[...], block, NN, preferred_element_type=F32)
        copies[k].wait()
        part = part + cross[k].astype(F32)
        if k:
            stage[k - 1] = part.astype(BF16)
            src, dst = stage.at[k - 1], rest[k - 1]
        else:
            own[...] = part
            src, dst = own, first
        outs.append(pltpu.make_async_copy(src, dst, out_sems.at[k]))
        outs[-1].start()
    for c in outs:
        c.wait()


def k_early(recv, keep, *refs):
    sends, held = refs[:-1], refs[-1]
    value = recv[0].astype(F32)
    for k in range(1, recv.shape[0]):
        value = value + recv[k].astype(F32)
    held[...] = value
    rows, nx = keep.shape[0], len(sends) + 1
    for k, out in enumerate((keep, *sends)):
        at = lax.rem(lax.axis_index("x") + k, nx) * rows
        out[...] = held[pl.ds(pl.multiple_of(at, 16), rows), :].astype(out.dtype)


def k_join(n, one, keep, *refs):
    out = refs[-1]
    width = out.shape[1] // n
    first = one[0].astype(F32)
    for k in range(1, one.shape[0]):
        first = first + one[k].astype(F32)
    second = keep[...]
    for r in refs[:-1]:
        second = second + r[...].astype(F32)
    for value, pieces in ((first.astype(BF16), by_x(n)), (second.astype(BF16), by_z())):
        for i, p in enumerate(pieces):
            out[:, span(source(n // 2, p), width)] = value[:, i * width : (i + 1) * width]


def k_add(first, *refs):
    value = first[...]
    for r in refs[:-1]:
        value = value + r[...].astype(F32)
    refs[-1][...] = value.astype(BF16).reshape(refs[-1].shape)


def call(body, outs, *args, limit=SMALL, flops=0, hbm_in=(), hbm_out=(), alias=None, scratch=()):
    spec, far = pl.BlockSpec(memory_space=pltpu.VMEM), pl.BlockSpec(memory_space=pltpu.HBM)
    ins = [far if i in hbm_in else spec for i in range(len(args))]
    size = sum(a.size * a.dtype.itemsize for a in args)
    return pl.pallas_call(
        body,
        out_shape=[
            pltpu.HBM(s, d) if i in hbm_out else jax.ShapeDtypeStruct(s, d)
            for i, (s, d) in enumerate(outs)
        ],
        in_specs=ins,
        out_specs=[far if i in hbm_out else spec for i in range(len(outs))],
        input_output_aliases=alias or {},
        scratch_shapes=list(scratch),
        compiler_params=pltpu.CompilerParams(vmem_limit_bytes=limit),
        cost_estimate=pl.CostEstimate(flops=flops, bytes_accessed=size, transcendentals=0),
    )(*args)


def shift(value, axis, step):
    n = lax.axis_size(axis)
    return lax.ppermute(value, axis, [(i, (i + step) % n) for i in range(n)])


def shards(embeddings, centroids, plan_grad):
    rows, width = embeddings.shape
    cols, depth = centroids.shape
    ny, nx, nz = lax.axis_size("y"), lax.axis_size("x"), lax.axis_size("z")
    nclus, nprog = ny * 2, nz * nx
    scale = 1.0 / (0.25 * float(depth) ** 0.5)
    ratio = (rows * nprog) / (cols * nclus)
    log_b = math.log(ratio)
    rv, cv = (rows // L, L), (cols // L, L)

    half = rows // 2
    left, right = shift(embeddings, "y", 1), shift(embeddings, "y", ny - 1)
    opposite = [shift(left[:half], "y", 1), shift(right[half:], "y", ny - 1)]
    mine = [[embeddings], [left], opposite, [right]]
    theirs = [[shift(m, "core", 1) for m in blocks] for blocks in mine]
    (grad,) = call(k_prepare, [((cols, rows), BF16)], plan_grad)
    mine[0][0], grad = lax.optimization_barrier((mine[0][0], grad))
    counts = [len(blocks) for blocks in (*mine, *theirs)]
    pieces = [m for blocks in (*mine, *theirs) for m in blocks]

    def over_clus(send):
        return lax.all_to_all(send, ("y", "core"), 0, 0, tiled=True)

    def over_prog(send):
        return lax.all_to_all(send, ("z", "x"), 0, 0, tiled=True)

    block = ((cols, rows), F32)
    row_send, col_send = ((nclus, *rv), F32), ((nprog, *cv), F32)
    row_pair, col_pair = ((nclus, 2, *rv), F32), ((nprog, 2, *cv), F32)
    a_row, a_col = (rv, F32), (cv, F32)

    work = 2 * rows * cols * depth
    logits, send, whole = call(
        functools.partial(k_logits, scale, counts),
        [block, row_pair, ((rows, depth), BF16)],
        centroids, *pieces,
        limit=LARGE, flops=work, hbm_out=(2,),
        scratch=[pltpu.VMEM((rows, depth), BF16), pltpu.SemaphoreType.DMA],
    )
    row_pot, send = call(k_first_col, [a_row, col_pair], logits, over_clus(send))
    col_pot, weights, send = call(
        functools.partial(k_weights, log_b), [a_col, block, row_send], logits, row_pot, over_prog(send)
    )
    row_mul, col_mul = [], []
    for step in range(1, ITERS):
        recv = over_clus(send)
        if step < ITERS - 1:
            a, send = call(k_col, [a_row, col_send], weights, recv)
            b, send = call(
                functools.partial(k_row, ratio), [a_col, row_send], weights, over_prog(send)
            )
            col_mul.append(b)
        else:
            a, send = call(k_last_col, [a_row, col_pair], weights, grad, recv)
        row_mul.append(a)
    b, x, send = call(
        functools.partial(k_adj_row, ratio),
        [a_col, a_col, row_send],
        weights, grad, over_prog(send),
    )
    col_mul.append(b)
    col_adj, row_adj = [x], []
    for step in range(ITERS - 1, 0, -1):
        y, send = call(
            functools.partial(k_back_col, 1.0 if step == ITERS - 1 else -1.0),
            [a_row, col_send],
            weights, row_mul[step - 1], over_clus(send),
        )
        row_adj.insert(0, y)
        b = col_mul[step - 2 : step - 1] if step > 1 else []
        x, send = call(
            functools.partial(k_back_row, ratio), [a_col, row_send], weights, *b, over_prog(send)
        )
        col_adj.insert(0, x)

    recv = over_clus(send)
    base, first = call(
        k_known,
        [block, ((cols, rows), BF16)],
        weights, grad, col_pot, *row_mul, *col_mul, *col_adj, *row_adj,
        flops=work, alias={0: 0, 1: 1},
    )
    per, n = cols // nx, len(counts)
    adjoint, turned = call(
        k_adjoint,
        [((cols, rows), BF16), ((rows, cols), BF16)],
        base, first, recv,
    )
    wide, narrow = len(by_x(n)) * width, len(by_z()) * width
    straight, near, *parts = call(
        functools.partial(k_cent, scale, n, nx),
        [((nz, cols // nz, narrow), BF16), ((per, wide), F32)]
        + [((per, wide), BF16)] * (nx - 1),
        adjoint, pltpu.with_memory_space_constraint(whole, pltpu.HBM),
        limit=LARGE, flops=work, hbm_in=(1,), hbm_out=range(1 + nx),
        scratch=[
            pltpu.VMEM((n, rows, width), BF16),
            pltpu.VMEM((cols, rows), BF16),
            pltpu.VMEM((len(by_x(n)), nx - 1, per, width), BF16),
            pltpu.VMEM((len(by_x(n)), per, width), F32),
            pltpu.VMEM((len(by_z()), nz, cols // nz, width), BF16),
            pltpu.SemaphoreType.DMA((n * nx,)),
            pltpu.SemaphoreType.DMA((n,)),
        ],
    )
    parts = [shift(p, "x", k + 1) for k, p in enumerate(parts)]
    cross, turned = call(
        functools.partial(k_cross, scale),
        [((ny, rows, width), BF16), ((rows, cols), BF16)],
        turned, centroids,
        limit=LARGE, flops=work // 2, hbm_out=(0, 1),
        scratch=[pltpu.VMEM((ny, rows, width), BF16), pltpu.SemaphoreType.DMA((ny + 1,))],
    )
    cross = shift(cross, "core", 1)
    straight = lax.all_to_all(straight, "z", 0, 0, tiled=True)
    own, *moved = call(
        functools.partial(k_pair, scale),
        [((rows, width), F32)] + [((rows, width), BF16)] * (ny - 1),
        pltpu.with_memory_space_constraint(turned, pltpu.HBM), centroids,
        pltpu.with_memory_space_constraint(cross, pltpu.HBM),
        limit=LARGE, flops=work // 2, hbm_in=(0, 2), hbm_out=range(ny),
        scratch=[
            pltpu.VMEM((rows, cols), BF16),
            pltpu.VMEM((ny, rows, width), BF16),
            pltpu.VMEM((rows, width), F32),
            pltpu.VMEM((ny - 1, rows, width), BF16),
            pltpu.SemaphoreType.DMA((ny + 1,)),
            pltpu.SemaphoreType.DMA((ny,)),
        ],
    )
    near, own = lax.optimization_barrier((near, own))
    moved = [shift(m, "y", k + 1) for k, m in enumerate(moved)]
    (parts,) = call(k_add, [((nz, per // nz, wide), BF16)], near, *parts, limit=LARGE)
    parts = lax.all_to_all(parts, "z", 0, 0, tiled=True)
    final = per // nz
    last, *late = call(
        k_early,
        [((final, narrow), F32)] + [((final, narrow), BF16)] * (nx - 1),
        straight,
        limit=LARGE, scratch=[pltpu.VMEM((cols // nz, narrow), F32)],
    )
    late = [shift(p, "x", k + 1) for k, p in enumerate(late)]
    (embed_grad,) = call(k_add, [((rows, width), BF16)], own, *moved, limit=LARGE)
    (centroid_grad,) = call(
        functools.partial(k_join, n), [((final, depth), BF16)], parts, last, *late, limit=LARGE
    )
    return embed_grad, centroid_grad


def solution(mesh):
    shape = dict(mesh.shape)
    nx = 4 if shape["prog"] % 4 == 0 and shape["prog"] > 4 else 2
    grid = (shape["prog"] // nx, nx, shape["clus"] // 2, 2)
    fine = Mesh(mesh.devices.reshape(grid), ("z", "x", "y", "core"))
    prog, clus = ("z", "x"), ("y", "core")
    return jax.shard_map(
        shards,
        mesh=fine,
        in_specs=(P(prog, clus), P(clus, None), P(prog, clus)),
        out_specs=(P(prog, clus), P(clus + prog, None)),
        check_vma=False,
    )
```

```python
import functools
import math

import jax
import jax.numpy as jnp
from jax import lax
from jax.experimental import pallas as pl
from jax.experimental.pallas import tpu as pltpu
from jax.sharding import Mesh
from jax.sharding import PartitionSpec as P


ITERS = 4
L = 128
F32 = jnp.float32
BF16 = jnp.bfloat16
NT = (((1,), (1,)), ((), ()))
NN = (((1,), (0,)), ((), ()))
SMALL = 12 << 20
LARGE = 40 << 20


def spread(vec):
    parts = [jnp.broadcast_to(vec[q : q + 1, :], (L, L)).T for q in range(vec.shape[0])]
    return jnp.concatenate(parts, axis=0)


def put_rows(out, parts):
    whole = jnp.concatenate(parts, axis=0)
    out[...] = jnp.broadcast_to(whole[None], out.shape)


def row_sums(values):
    return [jnp.sum(v, axis=0, keepdims=True) for v in values]


def gather_cols(part):
    return jnp.concatenate(
        [
            jnp.sum(part[q * L : (q + 1) * L, :].T, axis=0, keepdims=True)
            for q in range(part.shape[0] // L)
        ],
        axis=0,
    )


def first_lane(part):
    return jnp.concatenate(
        [part[q * L : (q + 1) * L, :].T[0:1, :] for q in range(part.shape[0] // L)], axis=0
    )


def lanes(ref, r):
    return ref[:, r * L : (r + 1) * L]


def total(recv):
    return jnp.sum(recv[...].astype(F32), axis=0)


def put_cols(out, part):
    out[...] = jnp.broadcast_to(gather_cols(part)[None], out.shape).astype(out.dtype)


def merge(recv):
    tops = recv[:, 0]
    top = jnp.max(tops, axis=0)
    return top + jnp.log(jnp.sum(recv[:, 1] * jnp.exp(tops - top[None]), axis=0))


def k_prepare(plan_grad, grad):
    grad[...] = plan_grad[...].T


def source(ny, k):
    core = lax.axis_index("core") if k < ny else 1 - lax.axis_index("core")
    return lax.rem(lax.axis_index("y") + (ny - k % ny), ny) * 2 + core


def target(ny, k, cross):
    core = 1 - lax.axis_index("core") if cross else lax.axis_index("core")
    return lax.rem(lax.axis_index("y") + k, ny) * 2 + core


def by_z():
    return (0,)


def by_x(n):
    return tuple(k for k in range(n) if k not in by_z())


def span(at, width):
    return pl.ds(pl.multiple_of(at * width, L), width)


def grouped(refs, counts):
    out, at = [], 0
    for c in counts:
        out.append(refs[at : at + c])
        at += c
    return out


def k_logits(scale, counts, cent, *refs):
    n = len(counts)
    pieces, (logits, send, whole, held, sems) = grouped(refs, counts), refs[sum(counts) :]
    copies = []
    for k, blocks in enumerate(pieces):
        at = 0
        for block in blocks:
            size = block.shape[0]
            copies.append(
                pltpu.make_async_copy(
                    block, whole.at[k, pl.ds(at, size), :], sems.at[len(copies)]
                )
            )
            copies[-1].start()
            held[at : at + size, span(source(n // 2, k), block.shape[1])] = block[...]
            at += size
    logits[...] = scale * lax.dot_general(cent[...], held[...], NT, preferred_element_type=F32)
    count = logits.shape[1] // L
    tops, sums = [], []
    for r in range(count):
        tile = lanes(logits, r)
        top = jnp.max(tile, axis=0, keepdims=True)
        tops.append(top)
        sums.append(jnp.sum(jnp.exp(tile - top), axis=0, keepdims=True))
    send[:, 0] = jnp.broadcast_to(jnp.concatenate(tops, axis=0)[None], send[:, 0].shape)
    send[:, 1] = jnp.broadcast_to(jnp.concatenate(sums, axis=0)[None], send[:, 1].shape)
    for c in copies:
        c.wait()


def k_first_col(logits, recv, row_pot, send):
    u = -merge(recv)
    row_pot[...] = u
    count = u.shape[0]
    top = lanes(logits, 0) + u[0:1, :]
    for r in range(1, count):
        top = jnp.maximum(top, lanes(logits, r) + u[r : r + 1, :])
    top = jnp.broadcast_to(jnp.max(top, axis=1, keepdims=True), top.shape)
    part = jnp.exp(lanes(logits, 0) + u[0:1, :] - top)
    for r in range(1, count):
        part = part + jnp.exp(lanes(logits, r) + u[r : r + 1, :] - top)
    send[:, 0] = jnp.broadcast_to(first_lane(top)[None], send[:, 0].shape)
    send[:, 1] = jnp.broadcast_to(gather_cols(part)[None], send[:, 1].shape)


def k_weights(log_b, logits, row_pot, recv, col_pot, weights, send):
    v = log_b - merge(recv)
    col_pot[...] = v
    vv = spread(v)
    u = row_pot[...]
    out = []
    for r in range(u.shape[0]):
        tile = jnp.exp(lanes(logits, r) + u[r : r + 1, :] + vv)
        weights[:, r * L : (r + 1) * L] = tile
        out.append(jnp.sum(tile, axis=0, keepdims=True))
    put_rows(send, out)


def weighted(weights, vec):
    part = lanes(weights, 0) * vec[0:1, :]
    for r in range(1, vec.shape[0]):
        part = part + lanes(weights, r) * vec[r : r + 1, :]
    return part


def k_col(weights, recv, row_mul, send):
    a = 1.0 / total(recv)
    row_mul[...] = a
    put_cols(send, weighted(weights, a))


def k_row(ratio, weights, recv, col_mul, send):
    b = ratio / total(recv)
    col_mul[...] = b
    bb = spread(b)
    count = weights.shape[1] // L
    put_rows(send, row_sums([lanes(weights, r) * bb for r in range(count)]))


def k_last_col(weights, grad, recv, row_mul, send):
    a = 1.0 / total(recv)
    row_mul[...] = a
    part = lanes(weights, 0) * a[0:1, :]
    bar = part * lanes(grad, 0).astype(F32)
    for r in range(1, a.shape[0]):
        step = lanes(weights, r) * a[r : r + 1, :]
        part = part + step
        bar = bar + step * lanes(grad, r).astype(F32)
    both = jnp.stack([gather_cols(part), gather_cols(bar)])
    send[...] = jnp.broadcast_to(both[None], send.shape).astype(send.dtype)


def k_adj_row(ratio, weights, grad, recv, col_mul, col_adj, send):
    sums = total(recv)
    b = ratio / sums[0]
    x = b * (b * sums[1]) / ratio
    col_mul[...] = b
    col_adj[...] = x
    bb, xx = spread(b), spread(x)
    count = weights.shape[1] // L
    put_rows(
        send,
        row_sums(
            [lanes(weights, r) * (bb * lanes(grad, r).astype(F32) - xx) for r in range(count)]
        ),
    )


def k_back_col(sign, weights, row_mul, recv, row_adj, send):
    a = row_mul[...]
    y = sign * a * a * total(recv)
    row_adj[...] = y
    put_cols(send, weighted(weights, y))


def k_back_row(ratio, weights, *refs):
    *col_mul, recv, col_adj, send = refs
    x = total(recv) / -ratio
    for b in col_mul:
        x = x * b[...] * b[...]
    col_adj[...] = x
    xx = spread(x)
    count = weights.shape[1] // L
    put_rows(send, row_sums([lanes(weights, r) * xx for r in range(count)]))


def k_known(weights, grad, col_pot, *refs):
    n = ITERS - 1
    base, first = refs[4 * n + 1 :]
    row_mul = [None] + [r[...] for r in refs[:n]]
    col_mul = [None, None] + [r[...] for r in refs[n : 2 * n]]
    x = [r[...] for r in refs[2 * n : 3 * n + 1]]
    y = [None] + [r[...] for r in refs[3 * n + 1 : 4 * n + 1]]
    b0 = spread(jnp.exp(-col_pot[...]))
    b4 = spread(col_mul[ITERS])
    xs = [spread(v) for v in x]
    bs = [None, None] + [spread(v) for v in col_mul[2:ITERS]]
    for r in range(base.shape[1] // L):
        row = slice(r, r + 1)
        tile = lanes(weights, r)
        inner = (b4 * row_mul[n][row, :]) * lanes(grad, r).astype(F32) - xs[0] - y[1][row, :]
        for t in range(1, ITERS):
            inner = inner - xs[t] * row_mul[t][row, :]
        for t in range(2, ITERS):
            inner = inner - bs[t] * y[t][row, :]
        first[:, r * L : (r + 1) * L] = (tile * b0).astype(BF16)
        base[:, r * L : (r + 1) * L] = tile * inner


def k_adjoint(base, first, recv, adjoint, turned):
    y = -total(recv)
    for r in range(y.shape[0]):
        tile = lanes(base, r) - lanes(first, r).astype(F32) * y[r : r + 1, :]
        tile = tile.astype(BF16)
        adjoint[:, r * L : (r + 1) * L] = tile
        turned[r * L : (r + 1) * L, :] = tile.T


def k_cent(scale, n, nx, adjoint, whole_hbm, straight, keep, *refs):
    sends, (whole, picked, wide, own, narrow, sems, in_sems) = refs[: nx - 1], refs[nx - 1 :]
    width = whole.shape[2]
    copies = [
        pltpu.make_async_copy(whole_hbm.at[p], whole.at[p], in_sems.at[p]) for p in range(n)
    ]
    for p in (*by_x(n), *by_z()):
        copies[p].start()
    per = keep.shape[0]
    group = 16
    for k in range(nx):
        to = lax.rem(lax.axis_index("x") + k, nx)
        for iz in range(per // group):
            at = pl.multiple_of((iz * nx + to) * group, group)
            picked[k * per + iz * group : k * per + (iz + 1) * group, :] = adjoint[pl.ds(at, group), :]
    outs = []

    def leave(src, dst):
        outs.append(pltpu.make_async_copy(src, dst, sems.at[len(outs)]))
        outs[-1].start()

    def product(left, p):
        copies[p].wait()
        return scale * lax.dot_general(left[...], whole[p], NN, preferred_element_type=F32)

    for i, p in enumerate(by_x(n)):
        part = product(picked, p)
        for k in range(1, nx):
            wide[i, k - 1] = part[k * per : (k + 1) * per, :].astype(BF16)
            leave(wide.at[i, k - 1], sends[k - 1].at[:, pl.ds(i * width, width)])
        own[i] = part[:per, :]
        leave(own.at[i], keep.at[:, pl.ds(i * width, width)])
    for i, p in enumerate(by_z()):
        part = product(adjoint, p)
        narrow[i] = part.astype(BF16).reshape(narrow.shape[1:])
        leave(narrow.at[i], straight.at[:, :, pl.ds(i * width, width)])
    for c in outs:
        c.wait()


def k_cross(scale, turned, cent, cross_hbm, turned_hbm, cross, sems):
    ny, _, width = cross.shape
    outs = [pltpu.make_async_copy(turned, turned_hbm, sems.at[ny])]
    outs[0].start()
    for k in range(ny):
        block = cent[:, span(target(ny, k, True), width)]
        part = scale * lax.dot_general(turned[...], block, NN, preferred_element_type=F32)
        cross[k] = part.astype(BF16)
        outs.append(pltpu.make_async_copy(cross.at[k], cross_hbm.at[k], sems.at[k]))
        outs[-1].start()
    for c in outs:
        c.wait()


def k_pair(scale, turned_hbm, cent, cross_hbm, *refs):
    ny = cross_hbm.shape[0]
    sends, (turned, cross, stage, sems, out_sems) = refs[: ny - 1], refs[ny - 1 :]
    width = cross.shape[2]
    bring = pltpu.make_async_copy(turned_hbm, turned, sems.at[0])
    bring.start()
    copies = [
        pltpu.make_async_copy(cross_hbm.at[k], cross.at[k - 1], sems.at[k]) for k in range(1, ny)
    ]
    for c in copies:
        c.start()
    bring.wait()
    outs = []
    for k in range(1, ny):
        block = cent[:, span(target(ny, k, False), width)]
        part = scale * lax.dot_general(turned[...], block, NN, preferred_element_type=F32)
        copies[k - 1].wait()
        stage[k - 1] = (part + cross[k - 1].astype(F32)).astype(BF16)
        outs.append(pltpu.make_async_copy(stage.at[k - 1], sends[k - 1], out_sems.at[k - 1]))
        outs[-1].start()
    for c in outs:
        c.wait()


def k_own(scale, turned, cent, cross, out):
    ny, width = cross.shape[0], cross.shape[2]
    block = cent[:, span(target(ny, 0, False), width)]
    part = scale * lax.dot_general(turned[...], block, NN, preferred_element_type=F32)
    out[...] = part + cross[0].astype(F32)


def k_early(recv, keep, *refs):
    sends, held = refs[:-1], refs[-1]
    value = recv[0].astype(F32)
    for k in range(1, recv.shape[0]):
        value = value + recv[k].astype(F32)
    held[...] = value
    rows, nx = keep.shape[0], len(sends) + 1
    for k, out in enumerate((keep, *sends)):
        at = lax.rem(lax.axis_index("x") + k, nx) * rows
        out[...] = held[pl.ds(pl.multiple_of(at, 16), rows), :].astype(out.dtype)


def k_join(n, one, keep, *refs):
    out = refs[-1]
    width = out.shape[1] // n
    first = one[0].astype(F32)
    for k in range(1, one.shape[0]):
        first = first + one[k].astype(F32)
    second = keep[...]
    for r in refs[:-1]:
        second = second + r[...].astype(F32)
    for value, pieces in ((first.astype(BF16), by_x(n)), (second.astype(BF16), by_z())):
        for i, p in enumerate(pieces):
            out[:, span(source(n // 2, p), width)] = value[:, i * width : (i + 1) * width]


def k_add(first, *refs):
    value = first[...]
    for r in refs[:-1]:
        value = value + r[...].astype(F32)
    refs[-1][...] = value.astype(BF16).reshape(refs[-1].shape)


def call(body, outs, *args, limit=SMALL, flops=0, hbm_in=(), hbm_out=(), alias=None, scratch=()):
    spec, far = pl.BlockSpec(memory_space=pltpu.VMEM), pl.BlockSpec(memory_space=pltpu.HBM)
    ins = [far if i in hbm_in else spec for i in range(len(args))]
    size = sum(a.size * a.dtype.itemsize for a in args)
    return pl.pallas_call(
        body,
        out_shape=[
            pltpu.HBM(s, d) if i in hbm_out else jax.ShapeDtypeStruct(s, d)
            for i, (s, d) in enumerate(outs)
        ],
        in_specs=ins,
        out_specs=[far if i in hbm_out else spec for i in range(len(outs))],
        input_output_aliases=alias or {},
        scratch_shapes=list(scratch),
        compiler_params=pltpu.CompilerParams(vmem_limit_bytes=limit),
        cost_estimate=pl.CostEstimate(flops=flops, bytes_accessed=size, transcendentals=0),
    )(*args)


def shift(value, axis, step):
    n = lax.axis_size(axis)
    return lax.ppermute(value, axis, [(i, (i + step) % n) for i in range(n)])


def shards(embeddings, centroids, plan_grad):
    rows, width = embeddings.shape
    cols, depth = centroids.shape
    ny, nx, nz = lax.axis_size("y"), lax.axis_size("x"), lax.axis_size("z")
    nclus, nprog = ny * 2, nz * nx
    scale = 1.0 / (0.25 * float(depth) ** 0.5)
    ratio = (rows * nprog) / (cols * nclus)
    log_b = math.log(ratio)
    rv, cv = (rows // L, L), (cols // L, L)

    half = rows // 2
    left, right = shift(embeddings, "y", 1), shift(embeddings, "y", ny - 1)
    opposite = [shift(left[:half], "y", 1), shift(right[half:], "y", ny - 1)]
    mine = [[embeddings], [left], opposite, [right]]
    theirs = [[shift(m, "core", 1) for m in blocks] for blocks in mine]
    (grad,) = call(k_prepare, [((cols, rows), BF16)], plan_grad)
    mine[0][0], grad = lax.optimization_barrier((mine[0][0], grad))
    counts = [len(blocks) for blocks in (*mine, *theirs)]
    pieces = [m for blocks in (*mine, *theirs) for m in blocks]

    def over_clus(send):
        return lax.all_to_all(send, ("y", "core"), 0, 0, tiled=True)

    def over_prog(send):
        return lax.all_to_all(send, ("z", "x"), 0, 0, tiled=True)

    block = ((cols, rows), F32)
    row_send, col_send = ((nclus, *rv), F32), ((nprog, *cv), F32)
    row_pair, col_pair = ((nclus, 2, *rv), F32), ((nprog, 2, *cv), F32)
    a_row, a_col = (rv, F32), (cv, F32)

    work = 2 * rows * cols * depth
    logits, send, whole = call(
        functools.partial(k_logits, scale, counts),
        [block, row_pair, ((len(counts), rows, width), BF16)],
        centroids, *pieces,
        limit=LARGE, flops=work, hbm_out=(2,),
        scratch=[pltpu.VMEM((rows, depth), BF16), pltpu.SemaphoreType.DMA((len(pieces),))],
    )
    row_pot, send = call(k_first_col, [a_row, col_pair], logits, over_clus(send))
    col_pot, weights, send = call(
        functools.partial(k_weights, log_b), [a_col, block, row_send], logits, row_pot, over_prog(send)
    )
    row_mul, col_mul = [], []
    for step in range(1, ITERS):
        recv = over_clus(send)
        if step < ITERS - 1:
            a, send = call(k_col, [a_row, col_send], weights, recv)
            b, send = call(
                functools.partial(k_row, ratio), [a_col, row_send], weights, over_prog(send)
            )
            col_mul.append(b)
        else:
            a, send = call(k_last_col, [a_row, col_pair], weights, grad, recv)
        row_mul.append(a)
    b, x, send = call(
        functools.partial(k_adj_row, ratio),
        [a_col, a_col, row_send],
        weights, grad, over_prog(send),
    )
    col_mul.append(b)
    col_adj, row_adj = [x], []
    for step in range(ITERS - 1, 0, -1):
        y, send = call(
            functools.partial(k_back_col, 1.0 if step == ITERS - 1 else -1.0),
            [a_row, col_send],
            weights, row_mul[step - 1], over_clus(send),
        )
        row_adj.insert(0, y)
        b = col_mul[step - 2 : step - 1] if step > 1 else []
        x, send = call(
            functools.partial(k_back_row, ratio), [a_col, row_send], weights, *b, over_prog(send)
        )
        col_adj.insert(0, x)

    recv = over_clus(send)
    base, first = call(
        k_known,
        [block, ((cols, rows), BF16)],
        weights, grad, col_pot, *row_mul, *col_mul, *col_adj, *row_adj,
        flops=work, alias={0: 0, 1: 1},
    )
    per, n = cols // nx, len(counts)
    adjoint, turned = call(
        k_adjoint,
        [((cols, rows), BF16), ((rows, cols), BF16)],
        base, first, recv,
    )
    wide, narrow = len(by_x(n)) * width, len(by_z()) * width
    straight, near, *parts = call(
        functools.partial(k_cent, scale, n, nx),
        [((nz, cols // nz, narrow), BF16), ((per, wide), F32)]
        + [((per, wide), BF16)] * (nx - 1),
        adjoint, pltpu.with_memory_space_constraint(whole, pltpu.HBM),
        limit=LARGE, flops=work, hbm_in=(1,), hbm_out=range(1 + nx),
        scratch=[
            pltpu.VMEM((n, rows, width), BF16),
            pltpu.VMEM((cols, rows), BF16),
            pltpu.VMEM((len(by_x(n)), nx - 1, per, width), BF16),
            pltpu.VMEM((len(by_x(n)), per, width), F32),
            pltpu.VMEM((len(by_z()), nz, cols // nz, width), BF16),
            pltpu.SemaphoreType.DMA((n * nx,)),
            pltpu.SemaphoreType.DMA((n,)),
        ],
    )
    parts = [shift(p, "x", k + 1) for k, p in enumerate(parts)]
    cross, turned = call(
        functools.partial(k_cross, scale),
        [((ny, rows, width), BF16), ((rows, cols), BF16)],
        turned, centroids,
        limit=LARGE, flops=work // 2, hbm_out=(0, 1),
        scratch=[pltpu.VMEM((ny, rows, width), BF16), pltpu.SemaphoreType.DMA((ny + 1,))],
    )
    cross = shift(cross, "core", 1)
    straight = lax.all_to_all(straight, "z", 0, 0, tiled=True)
    moved = call(
        functools.partial(k_pair, scale),
        [((rows, width), BF16)] * (ny - 1),
        pltpu.with_memory_space_constraint(turned, pltpu.HBM), centroids,
        pltpu.with_memory_space_constraint(cross, pltpu.HBM),
        limit=LARGE, flops=work // 2, hbm_in=(0, 2), hbm_out=range(ny - 1),
        scratch=[
            pltpu.VMEM((rows, cols), BF16),
            pltpu.VMEM((ny - 1, rows, width), BF16),
            pltpu.VMEM((ny - 1, rows, width), BF16),
            pltpu.SemaphoreType.DMA((ny,)),
            pltpu.SemaphoreType.DMA((ny - 1,)),
        ],
    )
    near, *moved = lax.optimization_barrier((near, *moved))
    moved = [shift(m, "y", k + 1) for k, m in enumerate(moved)]
    (own,) = call(
        functools.partial(k_own, scale),
        [((rows, width), F32)],
        turned, centroids, cross,
        limit=LARGE, flops=work // 8,
    )
    (parts,) = call(k_add, [((nz, per // nz, wide), BF16)], near, *parts, limit=LARGE)
    parts = lax.all_to_all(parts, "z", 0, 0, tiled=True)
    final = per // nz
    last, *late = call(
        k_early,
        [((final, narrow), F32)] + [((final, narrow), BF16)] * (nx - 1),
        straight,
        limit=LARGE, scratch=[pltpu.VMEM((cols // nz, narrow), F32)],
    )
    late = [shift(p, "x", k + 1) for k, p in enumerate(late)]
    (embed_grad,) = call(k_add, [((rows, width), BF16)], own, *moved, limit=LARGE)
    (centroid_grad,) = call(
        functools.partial(k_join, n), [((final, depth), BF16)], parts, last, *late, limit=LARGE
    )
    return embed_grad, centroid_grad


def solution(mesh):
    shape = dict(mesh.shape)
    nx = 4 if shape["prog"] % 4 == 0 and shape["prog"] > 4 else 2
    grid = (shape["prog"] // nx, nx, shape["clus"] // 2, 2)
    fine = Mesh(mesh.devices.reshape(grid), ("z", "x", "y", "core"))
    prog, clus = ("z", "x"), ("y", "core")
    return jax.shard_map(
        shards,
        mesh=fine,
        in_specs=(P(prog, clus), P(clus, None), P(prog, clus)),
        out_specs=(P(prog, clus), P(clus + prog, None)),
        check_vma=False,
    )
```

```python
import functools
import math

import jax
import jax.numpy as jnp
from jax import lax
from jax.experimental import pallas as pl
from jax.experimental.pallas import tpu as pltpu
from jax.sharding import Mesh
from jax.sharding import PartitionSpec as P


ITERS = 4
L = 128
F32 = jnp.float32
BF16 = jnp.bfloat16
NT = (((1,), (1,)), ((), ()))
NN = (((1,), (0,)), ((), ()))
SMALL = 12 << 20
LARGE = 40 << 20


def spread(vec):
    parts = [jnp.broadcast_to(vec[q : q + 1, :], (L, L)).T for q in range(vec.shape[0])]
    return jnp.concatenate(parts, axis=0)


def put_rows(out, parts):
    whole = jnp.concatenate(parts, axis=0)
    out[...] = jnp.broadcast_to(whole[None], out.shape)


def row_sums(values):
    return [jnp.sum(v, axis=0, keepdims=True) for v in values]


def gather_cols(part):
    return jnp.concatenate(
        [
            jnp.sum(part[q * L : (q + 1) * L, :].T, axis=0, keepdims=True)
            for q in range(part.shape[0] // L)
        ],
        axis=0,
    )


def first_lane(part):
    return jnp.concatenate(
        [part[q * L : (q + 1) * L, :].T[0:1, :] for q in range(part.shape[0] // L)], axis=0
    )


def lanes(ref, r):
    return ref[:, r * L : (r + 1) * L]


def total(recv):
    return jnp.sum(recv[...].astype(F32), axis=0)


def put_cols(out, part):
    out[...] = jnp.broadcast_to(gather_cols(part)[None], out.shape).astype(out.dtype)


def merge(recv):
    tops = recv[:, 0]
    top = jnp.max(tops, axis=0)
    return top + jnp.log(jnp.sum(recv[:, 1] * jnp.exp(tops - top[None]), axis=0))


def k_prepare(plan_grad, grad):
    grad[...] = plan_grad[...].T


def source(ny, k):
    core = lax.axis_index("core") if k < ny else 1 - lax.axis_index("core")
    return lax.rem(lax.axis_index("y") + (ny - k % ny), ny) * 2 + core


def target(ny, k, cross):
    core = 1 - lax.axis_index("core") if cross else lax.axis_index("core")
    return lax.rem(lax.axis_index("y") + k, ny) * 2 + core


def by_z(n):
    return (0, n // 2)


def by_x(n):
    return tuple(k for k in range(n) if k not in by_z(n))


def span(at, width):
    return pl.ds(pl.multiple_of(at * width, L), width)


def grouped(refs, counts):
    out, at = [], 0
    for c in counts:
        out.append(refs[at : at + c])
        at += c
    return out


def k_logits(scale, counts, cent, *refs):
    n = len(counts)
    pieces, (logits, send, whole, held, sem) = grouped(refs, counts), refs[sum(counts) :]
    for k, blocks in enumerate(pieces):
        at = 0
        for block in blocks:
            rows = slice(at, at + block.shape[0])
            held[rows, span(source(n // 2, k), block.shape[1])] = block[...]
            at += block.shape[0]
    copy = pltpu.make_async_copy(held, whole, sem)
    copy.start()
    logits[...] = scale * lax.dot_general(cent[...], held[...], NT, preferred_element_type=F32)
    count = logits.shape[1] // L
    tops, sums = [], []
    for r in range(count):
        tile = lanes(logits, r)
        top = jnp.max(tile, axis=0, keepdims=True)
        tops.append(top)
        sums.append(jnp.sum(jnp.exp(tile - top), axis=0, keepdims=True))
    send[:, 0] = jnp.broadcast_to(jnp.concatenate(tops, axis=0)[None], send[:, 0].shape)
    send[:, 1] = jnp.broadcast_to(jnp.concatenate(sums, axis=0)[None], send[:, 1].shape)
    copy.wait()


def k_first_col(logits, recv, row_pot, send):
    u = -merge(recv)
    row_pot[...] = u
    count = u.shape[0]
    top = lanes(logits, 0) + u[0:1, :]
    for r in range(1, count):
        top = jnp.maximum(top, lanes(logits, r) + u[r : r + 1, :])
    top = jnp.broadcast_to(jnp.max(top, axis=1, keepdims=True), top.shape)
    part = jnp.exp(lanes(logits, 0) + u[0:1, :] - top)
    for r in range(1, count):
        part = part + jnp.exp(lanes(logits, r) + u[r : r + 1, :] - top)
    send[:, 0] = jnp.broadcast_to(first_lane(top)[None], send[:, 0].shape)
    send[:, 1] = jnp.broadcast_to(gather_cols(part)[None], send[:, 1].shape)


def k_weights(log_b, logits, row_pot, recv, col_pot, weights, send):
    v = log_b - merge(recv)
    col_pot[...] = v
    vv = spread(v)
    u = row_pot[...]
    out = []
    for r in range(u.shape[0]):
        tile = jnp.exp(lanes(logits, r) + u[r : r + 1, :] + vv)
        weights[:, r * L : (r + 1) * L] = tile
        out.append(jnp.sum(tile, axis=0, keepdims=True))
    put_rows(send, out)


def weighted(weights, vec):
    part = lanes(weights, 0) * vec[0:1, :]
    for r in range(1, vec.shape[0]):
        part = part + lanes(weights, r) * vec[r : r + 1, :]
    return part


def k_col(weights, recv, row_mul, send):
    a = 1.0 / total(recv)
    row_mul[...] = a
    put_cols(send, weighted(weights, a))


def k_row(ratio, weights, recv, col_mul, send):
    b = ratio / total(recv)
    col_mul[...] = b
    bb = spread(b)
    count = weights.shape[1] // L
    put_rows(send, row_sums([lanes(weights, r) * bb for r in range(count)]))


def k_last_col(weights, grad, recv, row_mul, send):
    a = 1.0 / total(recv)
    row_mul[...] = a
    part = lanes(weights, 0) * a[0:1, :]
    bar = part * lanes(grad, 0).astype(F32)
    for r in range(1, a.shape[0]):
        step = lanes(weights, r) * a[r : r + 1, :]
        part = part + step
        bar = bar + step * lanes(grad, r).astype(F32)
    both = jnp.stack([gather_cols(part), gather_cols(bar)])
    send[...] = jnp.broadcast_to(both[None], send.shape).astype(send.dtype)


def k_adj_row(ratio, weights, grad, recv, col_mul, col_adj, send):
    sums = total(recv)
    b = ratio / sums[0]
    x = b * (b * sums[1]) / ratio
    col_mul[...] = b
    col_adj[...] = x
    bb, xx = spread(b), spread(x)
    count = weights.shape[1] // L
    put_rows(
        send,
        row_sums(
            [lanes(weights, r) * (bb * lanes(grad, r).astype(F32) - xx) for r in range(count)]
        ),
    )


def k_back_col(sign, weights, row_mul, recv, row_adj, send):
    a = row_mul[...]
    y = sign * a * a * total(recv)
    row_adj[...] = y
    put_cols(send, weighted(weights, y))


def k_back_row(ratio, weights, *refs):
    *col_mul, recv, col_adj, send = refs
    x = total(recv) / -ratio
    for b in col_mul:
        x = x * b[...] * b[...]
    col_adj[...] = x
    xx = spread(x)
    count = weights.shape[1] // L
    put_rows(send, row_sums([lanes(weights, r) * xx for r in range(count)]))


def k_known(weights, grad, col_pot, *refs):
    n = ITERS - 1
    base, first = refs[4 * n + 1 :]
    row_mul = [None] + [r[...] for r in refs[:n]]
    col_mul = [None, None] + [r[...] for r in refs[n : 2 * n]]
    x = [r[...] for r in refs[2 * n : 3 * n + 1]]
    y = [None] + [r[...] for r in refs[3 * n + 1 : 4 * n + 1]]
    b0 = spread(jnp.exp(-col_pot[...]))
    b4 = spread(col_mul[ITERS])
    xs = [spread(v) for v in x]
    bs = [None, None] + [spread(v) for v in col_mul[2:ITERS]]
    for r in range(base.shape[1] // L):
        row = slice(r, r + 1)
        tile = lanes(weights, r)
        inner = (b4 * row_mul[n][row, :]) * lanes(grad, r).astype(F32) - xs[0] - y[1][row, :]
        for t in range(1, ITERS):
            inner = inner - xs[t] * row_mul[t][row, :]
        for t in range(2, ITERS):
            inner = inner - bs[t] * y[t][row, :]
        first[:, r * L : (r + 1) * L] = (tile * b0).astype(BF16)
        base[:, r * L : (r + 1) * L] = tile * inner


def k_adjoint(scale, base, first, recv, cent_hbm, adjoint, turned_hbm, cross, cent, turned, sems):
    copy = pltpu.make_async_copy(cent_hbm, cent, sems.at[0])
    copy.start()
    y = -total(recv)
    for r in range(y.shape[0]):
        tile = lanes(base, r) - lanes(first, r).astype(F32) * y[r : r + 1, :]
        tile = tile.astype(BF16)
        adjoint[:, r * L : (r + 1) * L] = tile
        turned[r * L : (r + 1) * L, :] = tile.T
    back = pltpu.make_async_copy(turned, turned_hbm, sems.at[1])
    back.start()
    copy.wait()
    ny, _, width = cross.shape
    for k in range(ny):
        block = cent[:, span(target(ny, k, True), width)]
        part = scale * lax.dot_general(turned[...], block, NN, preferred_element_type=F32)
        cross[k] = part.astype(BF16)
    back.wait()


def k_cent(scale, n, nx, adjoint, whole, straight, keep, *refs):
    sends, (picked, wide, own, narrow, sems) = refs[: nx - 1], refs[nx - 1 :]
    width = whole.shape[1] // n
    per = keep.shape[0]
    group = 16
    for k in range(nx):
        to = lax.rem(lax.axis_index("x") + k, nx)
        for iz in range(per // group):
            at = pl.multiple_of((iz * nx + to) * group, group)
            picked[k * per + iz * group : k * per + (iz + 1) * group, :] = adjoint[pl.ds(at, group), :]
    outs = []

    def leave(src, dst):
        outs.append(pltpu.make_async_copy(src, dst, sems.at[len(outs)]))
        outs[-1].start()

    def product(left, p):
        right = whole[:, span(source(n // 2, p), width)]
        return scale * lax.dot_general(left[...], right, NN, preferred_element_type=F32)

    for i, p in enumerate(by_x(n)):
        part = product(picked, p)
        for k in range(1, nx):
            wide[i, k - 1] = part[k * per : (k + 1) * per, :].astype(BF16)
            leave(wide.at[i, k - 1], sends[k - 1].at[:, pl.ds(i * width, width)])
        own[i] = part[:per, :]
        leave(own.at[i], keep.at[:, pl.ds(i * width, width)])
    for i, p in enumerate(by_z(n)):
        part = product(adjoint, p)
        narrow[i] = part.astype(BF16).reshape(narrow.shape[1:])
        leave(narrow.at[i], straight.at[:, :, pl.ds(i * width, width)])
    for c in outs:
        c.wait()


def k_pair(scale, turned_hbm, cent, cross_hbm, *refs):
    ny = cross_hbm.shape[0]
    sends, (turned, cross, stage, sems, out_sems) = refs[: ny - 1], refs[ny - 1 :]
    width = cross.shape[2]
    bring = pltpu.make_async_copy(turned_hbm, turned, sems.at[0])
    bring.start()
    copies = [
        pltpu.make_async_copy(cross_hbm.at[k], cross.at[k - 1], sems.at[k]) for k in range(1, ny)
    ]
    for c in copies:
        c.start()
    bring.wait()
    outs = []
    for k in range(1, ny):
        block = cent[:, span(target(ny, k, False), width)]
        part = scale * lax.dot_general(turned[...], block, NN, preferred_element_type=F32)
        copies[k - 1].wait()
        stage[k - 1] = (part + cross[k - 1].astype(F32)).astype(BF16)
        outs.append(pltpu.make_async_copy(stage.at[k - 1], sends[k - 1], out_sems.at[k - 1]))
        outs[-1].start()
    for c in outs:
        c.wait()


def k_own(scale, turned, cent, cross, out):
    ny, width = cross.shape[0], cross.shape[2]
    block = cent[:, span(target(ny, 0, False), width)]
    part = scale * lax.dot_general(turned[...], block, NN, preferred_element_type=F32)
    out[...] = part + cross[0].astype(F32)


def k_early(recv, keep, *refs):
    sends, held = refs[:-1], refs[-1]
    value = recv[0].astype(F32)
    for k in range(1, recv.shape[0]):
        value = value + recv[k].astype(F32)
    held[...] = value
    rows, nx = keep.shape[0], len(sends) + 1
    for k, out in enumerate((keep, *sends)):
        at = lax.rem(lax.axis_index("x") + k, nx) * rows
        out[...] = held[pl.ds(pl.multiple_of(at, 16), rows), :].astype(out.dtype)


def k_join(n, one, keep, *refs):
    out = refs[-1]
    width = out.shape[1] // n
    first = one[0].astype(F32)
    for k in range(1, one.shape[0]):
        first = first + one[k].astype(F32)
    second = keep[...]
    for r in refs[:-1]:
        second = second + r[...].astype(F32)
    for value, pieces in ((first.astype(BF16), by_x(n)), (second.astype(BF16), by_z(n))):
        for i, p in enumerate(pieces):
            out[:, span(source(n // 2, p), width)] = value[:, i * width : (i + 1) * width]


def k_add(first, *refs):
    value = first[...]
    for r in refs[:-1]:
        value = value + r[...].astype(F32)
    refs[-1][...] = value.astype(BF16).reshape(refs[-1].shape)


def call(body, outs, *args, limit=SMALL, flops=0, hbm_in=(), hbm_out=(), alias=None, scratch=()):
    spec, far = pl.BlockSpec(memory_space=pltpu.VMEM), pl.BlockSpec(memory_space=pltpu.HBM)
    ins = [far if i in hbm_in else spec for i in range(len(args))]
    size = sum(a.size * a.dtype.itemsize for a in args)
    return pl.pallas_call(
        body,
        out_shape=[
            pltpu.HBM(s, d) if i in hbm_out else jax.ShapeDtypeStruct(s, d)
            for i, (s, d) in enumerate(outs)
        ],
        in_specs=ins,
        out_specs=[far if i in hbm_out else spec for i in range(len(outs))],
        input_output_aliases=alias or {},
        scratch_shapes=list(scratch),
        compiler_params=pltpu.CompilerParams(vmem_limit_bytes=limit),
        cost_estimate=pl.CostEstimate(flops=flops, bytes_accessed=size, transcendentals=0),
    )(*args)


def shift(value, axis, step):
    n = lax.axis_size(axis)
    return lax.ppermute(value, axis, [(i, (i + step) % n) for i in range(n)])


def shards(embeddings, centroids, plan_grad):
    rows, width = embeddings.shape
    cols, depth = centroids.shape
    ny, nx, nz = lax.axis_size("y"), lax.axis_size("x"), lax.axis_size("z")
    nclus, nprog = ny * 2, nz * nx
    scale = 1.0 / (0.25 * float(depth) ** 0.5)
    ratio = (rows * nprog) / (cols * nclus)
    log_b = math.log(ratio)
    rv, cv = (rows // L, L), (cols // L, L)

    half = rows // 2
    left, right = shift(embeddings, "y", 1), shift(embeddings, "y", ny - 1)
    opposite = [shift(left[:half], "y", 1), shift(right[half:], "y", ny - 1)]
    mine = [[embeddings], [left], opposite, [right]]
    theirs = [[shift(m, "core", 1) for m in blocks] for blocks in mine]
    (grad,) = call(k_prepare, [((cols, rows), BF16)], plan_grad)
    mine[0][0], grad = lax.optimization_barrier((mine[0][0], grad))
    counts = [len(blocks) for blocks in (*mine, *theirs)]
    pieces = [m for blocks in (*mine, *theirs) for m in blocks]

    def over_clus(send):
        return lax.all_to_all(send, ("y", "core"), 0, 0, tiled=True)

    def over_prog(send):
        return lax.all_to_all(send, ("z", "x"), 0, 0, tiled=True)

    block = ((cols, rows), F32)
    row_send, col_send = ((nclus, *rv), F32), ((nprog, *cv), F32)
    row_pair, col_pair = ((nclus, 2, *rv), F32), ((nprog, 2, *cv), F32)
    a_row, a_col = (rv, F32), (cv, F32)

    work = 2 * rows * cols * depth
    logits, send, whole = call(
        functools.partial(k_logits, scale, counts),
        [block, row_pair, ((rows, depth), BF16)],
        centroids, *pieces,
        limit=LARGE, flops=work, hbm_out=(2,),
        scratch=[pltpu.VMEM((rows, depth), BF16), pltpu.SemaphoreType.DMA],
    )
    row_pot, send = call(k_first_col, [a_row, col_pair], logits, over_clus(send))
    col_pot, weights, send = call(
        functools.partial(k_weights, log_b), [a_col, block, row_send], logits, row_pot, over_prog(send)
    )
    row_mul, col_mul = [], []
    for step in range(1, ITERS):
        recv = over_clus(send)
        if step < ITERS - 1:
            a, send = call(k_col, [a_row, col_send], weights, recv)
            b, send = call(
                functools.partial(k_row, ratio), [a_col, row_send], weights, over_prog(send)
            )
            col_mul.append(b)
        else:
            a, send = call(k_last_col, [a_row, col_pair], weights, grad, recv)
        row_mul.append(a)
    b, x, send = call(
        functools.partial(k_adj_row, ratio),
        [a_col, a_col, row_send],
        weights, grad, over_prog(send),
    )
    col_mul.append(b)
    col_adj, row_adj = [x], []
    for step in range(ITERS - 1, 0, -1):
        y, send = call(
            functools.partial(k_back_col, 1.0 if step == ITERS - 1 else -1.0),
            [a_row, col_send],
            weights, row_mul[step - 1], over_clus(send),
        )
        row_adj.insert(0, y)
        b = col_mul[step - 2 : step - 1] if step > 1 else []
        x, send = call(
            functools.partial(k_back_row, ratio), [a_col, row_send], weights, *b, over_prog(send)
        )
        col_adj.insert(0, x)

    recv = over_clus(send)
    base, first = call(
        k_known,
        [block, ((cols, rows), BF16)],
        weights, grad, col_pot, *row_mul, *col_mul, *col_adj, *row_adj,
        flops=work, alias={0: 0, 1: 1},
    )
    per, n = cols // nx, len(counts)
    adjoint, turned, cross = call(
        functools.partial(k_adjoint, scale),
        [((cols, rows), BF16), ((rows, cols), BF16), ((ny, rows, width), BF16)],
        base, first, recv, pltpu.with_memory_space_constraint(centroids, pltpu.HBM),
        limit=LARGE, flops=work // 2, hbm_in=(3,), hbm_out=(1,),
        scratch=[
            pltpu.VMEM((cols, depth), BF16),
            pltpu.VMEM((rows, cols), BF16),
            pltpu.SemaphoreType.DMA((2,)),
        ],
    )
    cross = shift(cross, "core", 1)
    wide, narrow = len(by_x(n)) * width, len(by_z(n)) * width
    straight, near, *parts = call(
        functools.partial(k_cent, scale, n, nx),
        [((nz, cols // nz, narrow), BF16), ((per, wide), F32)]
        + [((per, wide), BF16)] * (nx - 1),
        adjoint, whole,
        limit=LARGE, flops=work, hbm_out=range(1 + nx),
        scratch=[
            pltpu.VMEM((cols, rows), BF16),
            pltpu.VMEM((len(by_x(n)), nx - 1, per, width), BF16),
            pltpu.VMEM((len(by_x(n)), per, width), F32),
            pltpu.VMEM((len(by_z(n)), nz, cols // nz, width), BF16),
            pltpu.SemaphoreType.DMA((n * nx,)),
        ],
    )
    parts = [shift(p, "x", k + 1) for k, p in enumerate(parts)]
    straight = lax.all_to_all(straight, "z", 0, 0, tiled=True)
    moved = call(
        functools.partial(k_pair, scale),
        [((rows, width), BF16)] * (ny - 1),
        pltpu.with_memory_space_constraint(turned, pltpu.HBM), centroids,
        pltpu.with_memory_space_constraint(cross, pltpu.HBM),
        limit=LARGE, flops=work // 2, hbm_in=(0, 2), hbm_out=range(ny - 1),
        scratch=[
            pltpu.VMEM((rows, cols), BF16),
            pltpu.VMEM((ny - 1, rows, width), BF16),
            pltpu.VMEM((ny - 1, rows, width), BF16),
            pltpu.SemaphoreType.DMA((ny,)),
            pltpu.SemaphoreType.DMA((ny - 1,)),
        ],
    )
    near, *moved = lax.optimization_barrier((near, *moved))
    moved = [shift(m, "y", k + 1) for k, m in enumerate(moved)]
    (own,) = call(
        functools.partial(k_own, scale),
        [((rows, width), F32)],
        turned, centroids, cross,
        limit=60 << 20, flops=work // 8,
    )
    (parts,) = call(k_add, [((nz, per // nz, wide), BF16)], near, *parts, limit=LARGE)
    parts = lax.all_to_all(parts, "z", 0, 0, tiled=True)
    final = per // nz
    last, *late = call(
        k_early,
        [((final, narrow), F32)] + [((final, narrow), BF16)] * (nx - 1),
        straight,
        limit=LARGE, scratch=[pltpu.VMEM((cols // nz, narrow), F32)],
    )
    late = [shift(p, "x", k + 1) for k, p in enumerate(late)]
    (embed_grad,) = call(k_add, [((rows, width), BF16)], own, *moved, limit=LARGE)
    (centroid_grad,) = call(
        functools.partial(k_join, n), [((final, depth), BF16)], parts, last, *late, limit=LARGE
    )
    return embed_grad, centroid_grad


def solution(mesh):
    shape = dict(mesh.shape)
    nx = 4 if shape["prog"] % 4 == 0 and shape["prog"] > 4 else 2
    grid = (shape["prog"] // nx, nx, shape["clus"] // 2, 2)
    fine = Mesh(mesh.devices.reshape(grid), ("z", "x", "y", "core"))
    prog, clus = ("z", "x"), ("y", "core")
    return jax.shard_map(
        shards,
        mesh=fine,
        in_specs=(P(prog, clus), P(clus, None), P(prog, clus)),
        out_specs=(P(prog, clus), P(clus + prog, None)),
        check_vma=False,
    )
```
